256 devices in a mesh: dp: 8 (over x, core), grid: 32 (over y, z).
Axes of the slice: x: 4, y: 4, z: 8, core: 2. Of those that a mesh axis runs over, the one named last changes fastest.
Arguments:
- q_row: bfloat16 [16, 96, 96, 1536], P('dp', 'grid'), may hold values from -8 to 8, as said below
- k_row: bfloat16 [16, 96, 96, 1536], P('dp', 'grid'), may hold values from -8 to 8
- v_row: bfloat16 [16, 96, 96, 1536], P('dp', 'grid'), may hold values from -6 to 6
- q_col: bfloat16 [16, 96, 96, 1536], P('dp', None, 'grid'), may hold values from -8 to 8, as said below
- k_col: bfloat16 [16, 96, 96, 1536], P('dp', None, 'grid'), may hold values from -8 to 8
- cotangent: bfloat16 [16, 96, 96, 1536], P('dp', None, 'grid'), may hold values from -6 to 6
- w_value: bfloat16 [1536, 1536], P(('dp', 'grid')), may hold values from -0.15625 to 0.15625
- row_positions: int32 [96], replicated, may hold values from 0 to 95, each once
- col_positions: int32 [96], replicated, may hold values from 0 to 95, each once
- mlp_in: float32 [512], P('grid'), may hold values from -8 to 8
- mlp_bias: float32 [512], P('grid'), may hold values from -4 to 4
- mlp_out: float32 [512, 48], P('grid'), may hold values from -0.08 to 0.08
Outputs:
- attended: bfloat16 [16, 96, 96, 1536], P('dp', None, 'grid')
- grad_mlp_in: float32 [512], P('grid')
- grad_mlp_bias: float32 [512], P('grid')
- grad_mlp_out: float32 [512, 48], P('grid')
The draws below stay inside these ranges and needn't reach their ends.
Inputs may be any that keep to these rules, and one draw needn't show every extreme that they name: q_row and k_row lie within the range. q_col and k_col lie within the range. `row_positions`: each of 0 to 95 appears once. `col_positions`: each of 0 to 95 appears once.
All inputs are finite; a program needn't handle non-finite values.
Results may differ from the reference program's by a relative error of at most 0.007.
Values may be sent and summed in bfloat16 or wider, within the bound.
No kernel may reach another device: no remote copies, remote signals or barrier semaphores. Data moves between devices by JAX's collectives and lax.ppermute only.
A program may use at most 192 MiB of HBM per device.

```python
import jax
import jax.numpy as jnp
from jax import lax

G = 96
D = 1536
NH = 48
HD = 32
HM = 512
NOFF = 191
BATCH = 16


def draw_attention_pair(key):
    shape = (BATCH, G, G, D)
    key_out = jnp.clip(jax.random.normal(jax.random.fold_in(key, 31), shape, jnp.float32), -6.0, 6.0)
    query_out = jnp.clip(jax.random.normal(jax.random.fold_in(key, 32), shape, jnp.float32), -6.0, 6.0)
    return (query_out, key_out)


def draw_q_row(key, part):
    return draw_attention_pair(jax.random.fold_in(key, 1))[0].astype(jnp.bfloat16)


def draw_k_row(key, part):
    return draw_attention_pair(jax.random.fold_in(key, 1))[1].astype(jnp.bfloat16)


def draw_q_col(key, part):
    return draw_attention_pair(jax.random.fold_in(key, 2))[0].astype(jnp.bfloat16)


def draw_k_col(key, part):
    return draw_attention_pair(jax.random.fold_in(key, 2))[1].astype(jnp.bfloat16)


def block_scale(own_key, dims, split, least, high):
    def one(axis_at, blocks):
        steps = jax.random.uniform(jax.random.fold_in(jax.random.fold_in(own_key, 6), axis_at), (blocks,), jnp.float32, least / len(split), high / len(split))
        return jnp.repeat(jnp.exp(steps), dims[axis_at] // blocks).reshape((-1,) + (1,) * (len(dims) - axis_at - 1))

    level = one(*split[0])
    for cut in split[1:]:
        level = level * one(*cut)
    return level


def scatter_about(stream_key, extent, scale, limit, pieces=(), held_as=jnp.bfloat16):
    array = jax.random.normal(stream_key, extent, jnp.float32) * scale
    if len(pieces) > 0:
        array = block_scale(stream_key, extent, pieces, -0.22, 0.18) * array
    return jnp.clip(array, min=-limit, max=limit).astype(held_as)


def setup_inputs(seed: int = 0) -> dict:
    keys = jax.random.split(jax.random.key(seed), 13)
    return {
        "q_row": draw_q_row(jax.random.fold_in(keys[12], 71), 0),
        "k_row": draw_k_row(jax.random.fold_in(keys[12], 71), 0),
        "v_row": scatter_about(keys[2], (BATCH, G, G, D), 1.0, 6.0, ((0, 8), (1, 32))),
        "q_col": draw_q_col(jax.random.fold_in(keys[12], 71), 0),
        "k_col": draw_k_col(jax.random.fold_in(keys[12], 71), 0),
        "cotangent": scatter_about(keys[5], (BATCH, G, G, D), 1.0, 6.0, ((0, 8), (2, 32))),
        "w_value": scatter_about(keys[6], (D, D), D ** -0.5, 0.15625, ((0, 256),)),
        "row_positions": jax.random.permutation(keys[7], G).astype(jnp.int32),
        "col_positions": jax.random.permutation(keys[8], G).astype(jnp.int32),
        "mlp_in": scatter_about(keys[9], (HM,), 2.0, 8.0, ((0, 32),), jnp.float32),
        "mlp_bias": scatter_about(keys[10], (HM,), 1.0, 4.0, ((0, 32),), jnp.float32),
        "mlp_out": scatter_about(keys[11], (HM, NH), 0.013, 0.08, ((0, 32),), jnp.float32),
    }


PRECISE = lax.Precision.HIGHEST

def offset_coords():
    delta = jnp.arange(NOFF, dtype=jnp.float32) - (G - 1)
    scaled = delta * (8.0 / (G - 1))
    return jnp.sign(scaled) * jnp.log2(jnp.abs(scaled) + 1.0) / 3.0

def offset_one_hot(positions):
    spread = positions[:, None].astype(jnp.int32) - positions[None, :].astype(jnp.int32) + (G - 1)
    levels = jnp.arange(NOFF, dtype=jnp.int32)
    return (spread.reshape(-1)[:, None] == levels[None, :]).astype(jnp.float32)

def expand_bias(one_hot, bias_table):
    flat_bias = jnp.dot(one_hot, bias_table, precision=PRECISE)
    return flat_bias.reshape(G, G, NH).transpose(2, 0, 1)

def fold_bias(one_hot, bias_grad):
    flat_grad = bias_grad.transpose(1, 2, 0).reshape(G * G, NH)
    return lax.dot_general(one_hot, flat_grad, (((0,), (0,)), ((), ())), precision=PRECISE)

def soft_grad(attn_probs, d_probs):
    return attn_probs * (d_probs - lax.optimization_barrier(jnp.sum(attn_probs * d_probs, axis=-1, keepdims=True)))

def widen(narrow):
    return lax.optimization_barrier(narrow).astype(jnp.float32)

def reference(q_row, k_row, v_row, q_col, k_col, cotangent, w_value, row_positions, col_positions, mlp_in, mlp_bias, mlp_out):
    coords = offset_coords()
    pre_act = coords[:, None] * mlp_in[None, :] + mlp_bias[None, :]
    hidden_units = jnp.maximum(pre_act, 0.0)
    table_pre = jnp.dot(hidden_units, mlp_out, precision=PRECISE)
    squashed = jax.nn.sigmoid(table_pre)
    bias_table = 16.0 * squashed
    hot_cols = offset_one_hot(col_positions)
    hot_rows = offset_one_hot(row_positions)
    bias_row = expand_bias(hot_cols, bias_table)
    bias_col = expand_bias(hot_rows, bias_table)
    score_scale = HD ** (-0.5)

    def one_image(carry, items):
        row_query, row_key, row_value, col_query, col_key, grad_out = items
        query_rows = row_query.astype(jnp.float32).reshape(G, G, NH, HD)
        key_rows = row_key.astype(jnp.float32).reshape(G, G, NH, HD)
        value_rows = row_value.astype(jnp.float32).reshape(G, G, NH, HD)
        scores = jnp.einsum('nqhd,nkhd->nhqk', query_rows, key_rows) * score_scale + bias_row[None]
        p_row = jax.nn.softmax(scores, axis=-1)
        p_row_b = p_row.astype(jnp.bfloat16)
        row_out = jnp.einsum('nhqk,nkhd->nqhd', widen(p_row_b), value_rows).astype(jnp.bfloat16)
        projected = jnp.dot(row_out.reshape(G * G, D), w_value, preferred_element_type=jnp.float32)
        col_values = projected.astype(jnp.bfloat16)
        value_cols = widen(col_values).reshape(G, G, NH, HD)
        query_cols = col_query.astype(jnp.float32).reshape(G, G, NH, HD)
        key_cols = col_key.astype(jnp.float32).reshape(G, G, NH, HD)
        scores_col = jnp.einsum('qchd,kchd->chqk', query_cols, key_cols) * score_scale + bias_col[None]
        p_col = jax.nn.softmax(scores_col, axis=-1)
        p_col_w = widen(p_col.astype(jnp.bfloat16))
        attended = jnp.einsum('chqk,kchd->qchd', p_col_w, value_cols).astype(jnp.bfloat16).reshape(G, G, D)
        grad_cols = grad_out.astype(jnp.float32).reshape(G, G, NH, HD)
        dprob_col = jnp.einsum('qchd,kchd->chqk', grad_cols, value_cols)
        ds_col = soft_grad(p_col, dprob_col)
        d_values = jnp.einsum('chqk,qchd->kchd', p_col_w, grad_cols).astype(jnp.bfloat16).reshape(G * G, D)
        d_flat = lax.dot_general(d_values, w_value, (((1,), (1,)), ((), ())), preferred_element_type=jnp.float32)
        d_row_out = widen(d_flat.astype(jnp.bfloat16)).reshape(G, G, NH, HD)
        dprob_row = jnp.einsum('nqhd,nkhd->nhqk', d_row_out, value_rows)
        ds_row = soft_grad(p_row, dprob_row)
        return ((carry[0] + lax.optimization_barrier(jnp.sum(ds_row, axis=0)), carry[1] + lax.optimization_barrier(jnp.sum(ds_col, axis=0))), attended)
    start = (jnp.zeros((NH, G, G), jnp.float32), jnp.zeros((NH, G, G), jnp.float32))
    sums, attended = lax.scan(one_image, start, (q_row, k_row, v_row, q_col, k_col, cotangent))
    row_table = fold_bias(hot_cols, sums[0])
    col_table = fold_bias(hot_rows, sums[1])
    table_grad = (row_table + col_table) / (BATCH * G)
    pre_grad = table_grad * 16.0 * squashed * (1.0 - squashed)
    grad_mlp_out = lax.dot_general(hidden_units, pre_grad, (((0,), (0,)), ((), ())), precision=PRECISE)
    back_units = lax.dot_general(pre_grad, mlp_out, (((1,), (1,)), ((), ())), precision=PRECISE)
    unit_grad = jnp.where(pre_act > 0, back_units, 0.0)
    grad_mlp_in = lax.optimization_barrier(jnp.sum(unit_grad * coords[:, None], axis=0))
    grad_mlp_bias = lax.optimization_barrier(jnp.sum(unit_grad, axis=0))
    return (attended, grad_mlp_in, grad_mlp_bias, grad_mlp_out)
```

```python
import functools

import jax
import jax.numpy as jnp
import numpy as np
from jax import lax
from jax.experimental import pallas as pl
from jax.experimental.pallas import tpu as pltpu
from jax.sharding import PartitionSpec as P

G = 96
D = 1536
NH = 48
HD = 32
HM = 512
NOFF = 191
GRID = 32
DP = 8
LANES = 128
PACK = LANES // HD
GROUPS = D // LANES
ROWS = PACK * G
LOG2E = 1.4426950408889634

PRECISE = lax.Precision.HIGHEST
NT = (((1,), (1,)), ((), ()))
TN = (((0,), (0,)), ((), ()))
NN = (((1,), (0,)), ((), ()))

STACK = 2
UNROLL = GROUPS


def head_masks():
    lane = lax.broadcasted_iota(jnp.int32, (G, LANES), 1)
    return [(lane >= j * HD) & (lane < (j + 1) * HD) for j in range(PACK)]


def stack_heads(x, masks):
    zero = jnp.zeros_like(x)
    return jnp.concatenate([jnp.where(m, x, zero) for m in masks], axis=0)


def lane_group(g):
    return pl.ds(pl.multiple_of(g * LANES, LANES), LANES)


def head_rows(g, first):
    return pl.ds(pl.multiple_of(g * ROWS + first * G, G), STACK * G)


def softmax_rows(key, query, bias, masks):
    s = lax.dot_general(stack_heads(key, masks), query, NT, preferred_element_type=jnp.float32)
    s = s * (HD ** (-0.5) * LOG2E) + bias
    s = s.reshape(STACK, G, G)
    e = jnp.exp2(s - jnp.max(s, axis=1, keepdims=True))
    p = e * (1.0 / jnp.sum(e, axis=1, keepdims=True))
    return p.reshape(STACK * G, G).astype(jnp.bfloat16)


def forward_kernel(q_ref, k_ref, x_ref, bias_ref, p_ref, o_ref, *, transpose):
    masks = head_masks()

    def body(g, carry):
        sl = lane_group(g)
        query, key, x = q_ref[0, :, sl], k_ref[0, :, sl], x_ref[0, :, sl]
        o = None
        for first in range(0, PACK, STACK):
            own = masks[first:first + STACK]
            rows = head_rows(g, first)
            p = softmax_rows(key, query, bias_ref[rows, :G], own)
            p_ref[0, rows, :] = p
            if transpose:
                r = lax.dot_general(p, x, NN, preferred_element_type=jnp.float32)
                for j in range(STACK):
                    o = jnp.where(own[j], r[j * G:(j + 1) * G], 0.0 if o is None else o)
            else:
                r = lax.dot_general(
                    p, stack_heads(x, own), TN, preferred_element_type=jnp.float32
                )
                o = r if o is None else o + r
        o_ref[0, :, sl] = o.astype(jnp.bfloat16)
        return carry

    lax.fori_loop(0, GROUPS, body, 0, unroll=UNROLL)


def backward_kernel(p_ref, v_ref, g_ref, *outs, attend):
    sum_ref = outs[-1]
    masks = head_masks()

    @pl.when(pl.program_id(0) == 0)
    def _():
        sum_ref[...] = jnp.zeros_like(sum_ref)

    def body(g, carry):
        sl = lane_group(g)
        value, grad = v_ref[0, :, sl], g_ref[0, :, sl]
        o = None
        for first in range(0, PACK, STACK):
            rows = head_rows(g, first)
            vs = stack_heads(value, masks[first:first + STACK])
            p = p_ref[0, rows, :]
            if attend:
                r = lax.dot_general(p, vs, TN, preferred_element_type=jnp.float32)
                o = r if o is None else o + r
            dp = lax.dot_general(vs, grad, NT, preferred_element_type=jnp.float32)
            dp = dp.reshape(STACK, G, G)
            pf = p.astype(jnp.float32).reshape(STACK, G, G)
            ds = pf * (dp - jnp.sum(pf * dp, axis=1, keepdims=True))
            sum_ref[rows, :G] += ds.reshape(STACK * G, G)
        if attend:
            outs[0][0, :, sl] = o.astype(jnp.bfloat16)
        return carry

    lax.fori_loop(0, GROUPS, body, 0, unroll=UNROLL)


BLOCK = (1, G, D)
PSHAPE = (1, NH * G, G)


def each(shape):
    return pl.BlockSpec(shape, lambda i: (i, 0, 0))


def whole(shape):
    return pl.BlockSpec(shape, lambda i: (0,) * len(shape))


def attention_forward(q, k, x, bias, transpose):
    n = q.shape[0]
    return pl.pallas_call(
        functools.partial(forward_kernel, transpose=transpose),
        grid=(n,),
        in_specs=[each(BLOCK)] * 3 + [whole((NH * G, LANES))],
        out_specs=[each(PSHAPE), each(BLOCK)],
        out_shape=[
            jax.ShapeDtypeStruct((n, NH * G, G), jnp.bfloat16),
            jax.ShapeDtypeStruct((n, G, D), jnp.bfloat16),
        ],
        cost_estimate=pl.CostEstimate(flops=n * NH * 16 * G * G * LANES, transcendentals=n * NH * G * G, bytes_accessed=20_000_000),
    )(q, k, x, bias)


def attention_backward(p, v, g, attend):
    n = p.shape[0]
    specs = [each(BLOCK)] if attend else []
    shapes = [jax.ShapeDtypeStruct((n, G, D), jnp.bfloat16)] if attend else []
    return pl.pallas_call(
        functools.partial(backward_kernel, attend=attend),
        grid=(n,),
        in_specs=[each(PSHAPE), each(BLOCK), each(BLOCK)],
        out_specs=specs + [whole((NH * G, LANES))],
        out_shape=shapes + [jax.ShapeDtypeStruct((NH * G, LANES), jnp.float32)],
        cost_estimate=pl.CostEstimate(flops=n * NH * 16 * G * G * LANES, transcendentals=0, bytes_accessed=20_000_000),
    )(p, v, g)


def expand_kernel(pos_ref, table_ref, lane_ref, out_ref):
    low, high = table_ref[:, :LANES], table_ref[:, LANES:]
    lane = jnp.broadcast_to(lane_ref[...], (NH, LANES)) + (G - 1)

    def body(b, carry):
        level = lane - pos_ref[b]
        index = jnp.bitwise_and(level, LANES - 1)
        x = jnp.take_along_axis(low, index, axis=1, mode="promise_in_bounds")
        y = jnp.take_along_axis(high, index, axis=1, mode="promise_in_bounds")
        out_ref[pl.ds(b, NH, stride=G), :] = jnp.where(level >= LANES, y, x)
        return carry

    lax.fori_loop(0, G, body, 0, unroll=16)


def expand(table, positions):
    lane = jnp.pad(positions, (0, LANES - G))[None]
    return pl.pallas_call(
        expand_kernel,
        in_specs=[
            pl.BlockSpec(memory_space=pltpu.SMEM),
            pl.BlockSpec(memory_space=pltpu.VMEM),
            pl.BlockSpec(memory_space=pltpu.VMEM),
        ],
        out_specs=pl.BlockSpec(memory_space=pltpu.VMEM),
        out_shape=jax.ShapeDtypeStruct((NH * G, LANES), jnp.float32),
    )(positions, table, lane)


def fold_kernel(pos_ref, sum_ref, lane_ref, out_ref):
    lane = jnp.broadcast_to(lane_ref[...], (NH, LANES))
    keep = lax.broadcasted_iota(jnp.int32, (NH, LANES), 1) < G
    zero = jnp.zeros((NH, LANES), jnp.float32)

    def body(b, total):
        one = sum_ref[pl.ds(b, NH, stride=G), :]
        one = jnp.take_along_axis(one, lane, axis=1, mode="promise_in_bounds")
        one = jnp.concatenate([jnp.where(keep, one, 0.0), zero], axis=1)
        return total + pltpu.roll(one, (G - 1) - pos_ref[b], 1)

    out_ref[...] = lax.fori_loop(0, G, body, jnp.zeros((NH, 2 * LANES), jnp.float32), unroll=4)


def fold(sums, positions):
    inverse = jnp.sum(
        jnp.where(positions[None, :] == jnp.arange(LANES)[:, None], jnp.arange(G)[None, :], 0), axis=1
    ).astype(jnp.int32)[None]
    return pl.pallas_call(
        fold_kernel,
        in_specs=[
            pl.BlockSpec(memory_space=pltpu.SMEM),
            pl.BlockSpec(memory_space=pltpu.VMEM),
            pl.BlockSpec(memory_space=pltpu.VMEM),
        ],
        out_specs=pl.BlockSpec(memory_space=pltpu.VMEM),
        out_shape=jax.ShapeDtypeStruct((NH, 2 * LANES), jnp.float32),
    )(positions, sums, inverse)

def offset_coords():
    delta = jnp.arange(NOFF, dtype=jnp.float32) - (G - 1)
    scaled = delta * (8.0 / (G - 1))
    return jnp.sign(scaled) * jnp.log2(jnp.abs(scaled) + 1.0) / 3.0


def to_tile(flat):
    pad = [(0, 0)] * (flat.ndim - 1) + [(0, 1024 - flat.shape[-1])]
    return jnp.pad(flat, pad).reshape(flat.shape[:-1] + (8, 128))


def from_tile(tiles):
    return tiles.reshape(tiles.shape[:-2] + (1024,))[..., :800]


def gather_units(mlp_in, mlp_bias, mlp_out):
    own = jnp.concatenate([mlp_out, mlp_in[:, None], mlp_bias[:, None]], axis=1)
    tile = to_tile(own.reshape(800))
    got = lax.all_to_all(
        jnp.broadcast_to(tile[None], (GRID, 8, 128)), "grid", 0, 0, tiled=True
    )
    units = from_tile(got).reshape(HM, 50)
    return units[:, :NH], units[:, NH], units[:, NH + 1]


def reduce_units(grad_out, grad_in, grad_bias):
    whole = jnp.concatenate([grad_out, grad_in[:, None], grad_bias[:, None]], axis=1)
    tiles = to_tile(whole.reshape(GRID, 800))
    got = lax.all_to_all(tiles, "grid", 0, 0, tiled=True)
    own = jnp.sum(got, axis=0)
    got = lax.all_to_all(jnp.broadcast_to(own[None], (DP, 8, 128)), "dp", 0, 0, tiled=True)
    own = from_tile(jnp.sum(got, axis=0)).reshape(16, 50)
    return own[:, :NH], own[:, NH], own[:, NH + 1]


def along_x(step, swap):
    return [(i, ((i // 2 + step) % 4) * 2 + ((i % 2) ^ swap)) for i in range(DP)]


def fetch_weight(w_value):
    part = lax.all_to_all(
        jnp.broadcast_to(w_value[None], (GRID,) + w_value.shape), "grid", 0, 0, tiled=True
    ).reshape(D // DP, D)
    mine = [part]
    for step in (1, 2, 3):
        mine.append(lax.ppermute(part, "dp", along_x(step, 0)))
    mine = jnp.stack(mine)
    other = lax.ppermute(mine, "dp", along_x(0, 1))
    both = jnp.stack([mine, other])
    here = lax.axis_index("dp")
    x, core = here // 2, here % 2
    blocks = []
    for target in range(DP):
        tx, tc = target // 2, target % 2
        blocks.append(both[jnp.bitwise_xor(core, tc), (x - tx) % 4])
    return jnp.concatenate(blocks, axis=0)


def shards(
    q_row, k_row, v_row, q_col, k_col, cotangent, w_value,
    row_positions, col_positions, mlp_in, mlp_bias, mlp_out,
):
    images = q_row.shape[0]
    row_count = q_row.shape[1]
    col_count = q_col.shape[2]
    all_out, all_in, all_bias = gather_units(mlp_in, mlp_bias, mlp_out)
    coords = offset_coords()
    pre_act = coords[:, None] * all_in[None, :] + all_bias[None, :]
    hidden_units = jnp.maximum(pre_act, 0.0)
    table_pre = lax.dot_general(all_out, hidden_units, (((0,), (1,)), ((), ())), precision=PRECISE)
    squashed = jax.nn.sigmoid(table_pre)
    table = jnp.pad(squashed * (16.0 * LOG2E), ((0, 0), (0, 2 * LANES - NOFF)))
    whole_weight = fetch_weight(w_value)

    rows = lambda x: x.reshape(images * row_count, G, D)
    cols = lambda x: x.transpose(0, 2, 1, 3).reshape(images * col_count, G, D)
    bias_row = expand(table, col_positions)
    p_row, row_out = attention_forward(rows(q_row), rows(k_row), rows(v_row), bias_row, False)
    col_out = lax.all_to_all(
        row_out.reshape(images, row_count, G, D), "grid", split_axis=2, concat_axis=1, tiled=True
    )

    bias_col = expand(table, row_positions)
    grad_cols = cols(cotangent)
    p_col, d_values = attention_forward(cols(q_col), cols(k_col), grad_cols, bias_col, True)
    d_rows = lax.all_to_all(
        d_values.reshape(images, col_count, G, D), "grid", split_axis=2, concat_axis=1, tiled=True
    )

    value_cols = jnp.dot(
        cols(col_out).reshape(-1, D), whole_weight, preferred_element_type=jnp.float32
    ).astype(jnp.bfloat16).reshape(images * col_count, G, D)
    attended, col_sums = attention_backward(p_col, value_cols, grad_cols, True)
    attended = attended.reshape(images, col_count, G, D).transpose(0, 2, 1, 3)
    col_table = fold(col_sums, row_positions)

    d_flat = lax.dot_general(
        d_rows.transpose(0, 2, 1, 3).reshape(-1, D), whole_weight, NT,
        preferred_element_type=jnp.float32,
    )
    d_row_out = d_flat.astype(jnp.bfloat16).reshape(images * row_count, G, D)
    (row_sums,) = attention_backward(p_row, rows(v_row), d_row_out, False)
    row_table = fold(row_sums, col_positions)

    batch_size = lax.axis_size("dp") * images
    table_grad = (row_table + col_table)[:, :NOFF] / (batch_size * G)
    pre_grad = table_grad * 16.0 * squashed * (1.0 - squashed)
    grad_out = lax.dot_general(
        hidden_units, pre_grad, (((0,), (1,)), ((), ())), precision=PRECISE
    )
    back_units = lax.dot_general(pre_grad, all_out, (((0,), (1,)), ((), ())), precision=PRECISE)
    unit_grad = jnp.where(pre_act > 0, back_units, 0.0)
    grad_in = jnp.sum(unit_grad * coords[:, None], axis=0)
    grad_bias = jnp.sum(unit_grad, axis=0)
    grad_mlp_out, grad_mlp_in, grad_mlp_bias = reduce_units(grad_out, grad_in, grad_bias)
    return (attended, grad_mlp_in, grad_mlp_bias, grad_mlp_out)


def solution(mesh):
    return jax.shard_map(
        shards,
        mesh=mesh,
        in_specs=(
            P("dp", "grid", None, None),
            P("dp", "grid", None, None),
            P("dp", "grid", None, None),
            P("dp", None, "grid", None),
            P("dp", None, "grid", None),
            P("dp", None, "grid", None),
            P(("dp", "grid"), None),
            P(),
            P(),
            P("grid"),
            P("grid"),
            P("grid", None),
        ),
        out_specs=(P("dp", None, "grid", None), P("grid"), P("grid"), P("grid", None)),
        check_vma=False,
    )
```

```python
import functools

import jax
import jax.numpy as jnp
from jax import lax
from jax.experimental import pallas as pl
from jax.experimental.pallas import tpu as pltpu
from jax.sharding import PartitionSpec as P


G = 96
D = 1536
NH = 48
HD = 32
HM = 512
NOFF = 191
GRID = 32
DP = 8
LANES = 128
PACK = LANES // HD
GROUPS = D // LANES
ROWS = PACK * G
LOG2E = 1.4426950408889634

PRECISE = lax.Precision.HIGHEST
NT = (((1,), (1,)), ((), ()))
TN = (((0,), (0,)), ((), ()))
NN = (((1,), (0,)), ((), ()))

STACK = 2
UNROLL = GROUPS


def head_masks():
    lane = lax.broadcasted_iota(jnp.int32, (G, LANES), 1)
    return [(lane >= j * HD) & (lane < (j + 1) * HD) for j in range(PACK)]


def stack_heads(x, masks):
    zero = jnp.zeros_like(x)
    return jnp.concatenate([jnp.where(m, x, zero) for m in masks], axis=0)


def lane_group(g):
    return pl.ds(pl.multiple_of(g * LANES, LANES), LANES)


def head_rows(g, first):
    return pl.ds(pl.multiple_of(g * ROWS + first * G, G), STACK * G)


def softmax_rows(key, query, bias, masks):
    s = lax.dot_general(stack_heads(key, masks), query, NT, preferred_element_type=jnp.float32)
    s = s * (HD ** (-0.5) * LOG2E) + bias
    s = s.reshape(STACK, G, G)
    e = jnp.exp2(s - jnp.max(s, axis=1, keepdims=True))
    p = e * (1.0 / jnp.sum(e, axis=1, keepdims=True))
    return p.reshape(STACK * G, G).astype(jnp.bfloat16)


def pick(row, index):
    return jnp.take_along_axis(row, index, axis=1, mode="promise_in_bounds")


def forward_kernel(q_ref, k_ref, x_ref, table_ref, level_ref, p_ref, o_ref, bias_ref, *, transpose):
    masks = head_masks()

    @pl.when(pl.program_id(0) == 0)
    def _():
        level = level_ref[...]
        index = jnp.bitwise_and(level, LANES - 1)
        high = level >= LANES

        def spread(block, carry):
            table = table_ref[pl.ds(pl.multiple_of(block * 8, 8), 8), :]
            for j in range(8):
                low = jnp.broadcast_to(table[j:j + 1, :LANES], (G, LANES))
                up = jnp.broadcast_to(table[j:j + 1, LANES:], (G, LANES))
                rows = pl.ds(pl.multiple_of((block * 8 + j) * G, G), G)
                bias_ref[rows, :] = jnp.where(high, pick(up, index), pick(low, index))
            return carry

        lax.fori_loop(0, NH // 8, spread, 0)

    def body(g, carry):
        sl = lane_group(g)
        query, key, x = q_ref[0, :, sl], k_ref[0, :, sl], x_ref[0, :, sl]
        o = None
        for first in range(0, PACK, STACK):
            own = masks[first:first + STACK]
            rows = head_rows(g, first)
            p = softmax_rows(key, query, bias_ref[rows, :G], own)
            p_ref[0, rows, :] = p
            if transpose:
                r = lax.dot_general(p, x, NN, preferred_element_type=jnp.float32)
                for j in range(STACK):
                    o = jnp.where(own[j], r[j * G:(j + 1) * G], 0.0 if o is None else o)
            else:
                r = lax.dot_general(
                    p, stack_heads(x, own), TN, preferred_element_type=jnp.float32
                )
                o = r if o is None else o + r
        o_ref[0, :, sl] = o.astype(jnp.bfloat16)
        return carry

    lax.fori_loop(0, GROUPS, body, 0, unroll=UNROLL)


def backward_kernel(p_ref, v_ref, g_ref, index_ref, *outs, attend):
    fold_ref, sum_ref = outs[-2:]
    masks = head_masks()

    @pl.when(pl.program_id(0) == 0)
    def _():
        sum_ref[...] = jnp.zeros_like(sum_ref)

    def body(g, carry):
        sl = lane_group(g)
        value, grad = v_ref[0, :, sl], g_ref[0, :, sl]
        o = None
        for first in range(0, PACK, STACK):
            rows = head_rows(g, first)
            vs = stack_heads(value, masks[first:first + STACK])
            p = p_ref[0, rows, :]
            if attend:
                r = lax.dot_general(p, vs, TN, preferred_element_type=jnp.float32)
                o = r if o is None else o + r
            dp = lax.dot_general(vs, grad, NT, preferred_element_type=jnp.float32)
            dp = dp.reshape(STACK, G, G)
            pf = p.astype(jnp.float32).reshape(STACK, G, G)
            ds = pf * (dp - jnp.sum(pf * dp, axis=1, keepdims=True))
            sum_ref[rows, :G] += ds.reshape(STACK * G, G)
        if attend:
            outs[0][0, :, sl] = o.astype(jnp.bfloat16)
        return carry

    lax.fori_loop(0, GROUPS, body, 0, unroll=UNROLL)

    @pl.when(pl.program_id(0) == pl.num_programs(0) - 1)
    def _():
        low, high = index_ref[:, :LANES], index_ref[:, LANES:]

        def gather(block, carry):
            lows, highs = [], []
            for j in range(8):
                own = sum_ref[pl.ds(pl.multiple_of((block * 8 + j) * G, G), G), :]
                lows.append(jnp.sum(pick(own, low), axis=0, keepdims=True))
                highs.append(jnp.sum(pick(own, high), axis=0, keepdims=True))
            rows = pl.ds(pl.multiple_of(block * 8, 8), 8)
            fold_ref[rows, :LANES] = jnp.concatenate(lows, axis=0)
            fold_ref[rows, LANES:] = jnp.concatenate(highs, axis=0)
            return carry

        lax.fori_loop(0, NH // 8, gather, 0)


BLOCK = (1, G, D)
PSHAPE = (1, NH * G, G)


def each(shape):
    return pl.BlockSpec(shape, lambda i: (i, 0, 0))


def whole(shape):
    return pl.BlockSpec(shape, lambda i: (0,) * len(shape))


def attention_forward(q, k, x, table, level, transpose):
    n = q.shape[0]
    return pl.pallas_call(
        functools.partial(forward_kernel, transpose=transpose),
        grid=(n,),
        in_specs=[each(BLOCK)] * 3 + [whole((NH, 2 * LANES)), whole((G, LANES))],
        out_specs=[each(PSHAPE), each(BLOCK)],
        out_shape=[
            jax.ShapeDtypeStruct((n, NH * G, G), jnp.bfloat16),
            jax.ShapeDtypeStruct((n, G, D), jnp.bfloat16),
        ],
        scratch_shapes=[pltpu.VMEM((NH * G, LANES), jnp.float32)],
        cost_estimate=pl.CostEstimate(
            flops=n * NH * 16 * G * G * LANES, transcendentals=n * NH * G * G, bytes_accessed=20_000_000
        ),
    )(q, k, x, table, level)


def attention_backward(p, v, g, index, attend):
    n = p.shape[0]
    specs = [each(BLOCK)] if attend else []
    shapes = [jax.ShapeDtypeStruct((n, G, D), jnp.bfloat16)] if attend else []
    return pl.pallas_call(
        functools.partial(backward_kernel, attend=attend),
        grid=(n,),
        in_specs=[each(PSHAPE), each(BLOCK), each(BLOCK), whole((G, 2 * LANES))],
        out_specs=specs + [whole((NH, 2 * LANES))],
        out_shape=shapes + [jax.ShapeDtypeStruct((NH, 2 * LANES), jnp.float32)],
        scratch_shapes=[pltpu.VMEM((NH * G, LANES), jnp.float32)],
        cost_estimate=pl.CostEstimate(
            flops=n * NH * 16 * G * G * LANES, transcendentals=0, bytes_accessed=20_000_000
        ),
    )(p, v, g, index)


def levels(positions):
    level = positions[None, :] - positions[:, None] + (G - 1)
    return jnp.pad(level, ((0, 0), (0, LANES - G)))


def fold_index(positions):
    level = positions[None, :] - positions[:, None] + (G - 1)
    hit = level[:, :, None] == jnp.arange(2 * LANES)[None, None, :]
    spot = jnp.arange(G, dtype=jnp.int32)[None, :, None] - (LANES - 1)
    return jnp.sum(jnp.where(hit, spot, 0), axis=1) + (LANES - 1)


def assemble_kernel(start_ref, *refs):
    out_ref = refs[-1]
    for j in range(DP):
        first = pl.multiple_of(start_ref[j], D // DP)
        out_ref[pl.ds(first, D // DP), :] = refs[j][...]


def assemble(parts, starts):
    return pl.pallas_call(
        assemble_kernel,
        in_specs=[pl.BlockSpec(memory_space=pltpu.SMEM)] + [pl.BlockSpec(memory_space=pltpu.VMEM)] * DP,
        out_specs=pl.BlockSpec(memory_space=pltpu.VMEM),
        out_shape=jax.ShapeDtypeStruct((D, D), jnp.bfloat16),
        cost_estimate=pl.CostEstimate(flops=0, transcendentals=0, bytes_accessed=2 * D * D * 2),
    )(starts, *parts)


def offset_coords():
    delta = jnp.arange(NOFF, dtype=jnp.float32) - (G - 1)
    scaled = delta * (8.0 / (G - 1))
    return jnp.sign(scaled) * jnp.log2(jnp.abs(scaled) + 1.0) / 3.0


def to_tile(flat):
    pad = [(0, 0)] * (flat.ndim - 1) + [(0, 1024 - flat.shape[-1])]
    return jnp.pad(flat, pad).reshape(flat.shape[:-1] + (8, 128))


def from_tile(tiles):
    return tiles.reshape(tiles.shape[:-2] + (1024,))[..., :800]


def gather_units(mlp_in, mlp_bias, mlp_out):
    own = jnp.concatenate([mlp_out, mlp_in[:, None], mlp_bias[:, None]], axis=1)
    tile = to_tile(own.reshape(800))
    got = lax.all_to_all(
        jnp.broadcast_to(tile[None], (GRID, 8, 128)), "grid", 0, 0, tiled=True
    )
    units = from_tile(got).reshape(HM, 50)
    return units[:, :NH], units[:, NH], units[:, NH + 1]


def reduce_units(grad_out, grad_in, grad_bias):
    whole = jnp.concatenate([grad_out, grad_in[:, None], grad_bias[:, None]], axis=1)
    tiles = to_tile(whole.reshape(GRID, 800))
    got = lax.all_to_all(tiles, "grid", 0, 0, tiled=True)
    own = jnp.sum(got, axis=0)
    got = lax.all_to_all(jnp.broadcast_to(own[None], (DP, 8, 128)), "dp", 0, 0, tiled=True)
    own = from_tile(jnp.sum(got, axis=0)).reshape(16, 50)
    return own[:, :NH], own[:, NH], own[:, NH + 1]


def along_x(step, swap):
    return [(i, ((i // 2 + step) % 4) * 2 + ((i % 2) ^ swap)) for i in range(DP)]


def fetch_weight(w_value):
    part = lax.all_to_all(
        jnp.broadcast_to(w_value[None], (GRID,) + w_value.shape), "grid", 0, 0, tiled=True
    ).reshape(D // DP, D)
    mine = [part]
    for step in (1, 2, 3):
        mine.append(lax.ppermute(part, "dp", along_x(step, 0)))
    other = []
    for step in range(4):
        other.append(lax.ppermute(mine[step], "dp", along_x(0, 1)))
    here = lax.axis_index("dp")
    x, core = here // 2, here % 2
    order = (x - jnp.arange(4)) % 4 * 2
    starts = jnp.concatenate([order + core, order + (1 - core)]) * (D // DP)
    return assemble(mine + other, starts.astype(jnp.int32))


def shards(
    q_row, k_row, v_row, q_col, k_col, cotangent, w_value,
    row_positions, col_positions, mlp_in, mlp_bias, mlp_out,
):
    images = q_row.shape[0]
    row_count = q_row.shape[1]
    col_count = q_col.shape[2]
    all_out, all_in, all_bias = gather_units(mlp_in, mlp_bias, mlp_out)
    coords = offset_coords()
    pre_act = coords[:, None] * all_in[None, :] + all_bias[None, :]
    hidden_units = jnp.maximum(pre_act, 0.0)
    table_pre = lax.dot_general(all_out, hidden_units, (((0,), (1,)), ((), ())), precision=PRECISE)
    squashed = jax.nn.sigmoid(table_pre)
    table = jnp.pad(squashed * (16.0 * LOG2E), ((0, 0), (0, 2 * LANES - NOFF)))
    whole_weight = fetch_weight(w_value)

    rows = lambda x: x.reshape(images * row_count, G, D)
    cols = lambda x: x.transpose(0, 2, 1, 3).reshape(images * col_count, G, D)
    p_row, row_out = attention_forward(
        rows(q_row), rows(k_row), rows(v_row), table, levels(col_positions), False
    )
    col_out = lax.all_to_all(
        row_out.reshape(images, row_count, G, D), "grid", split_axis=2, concat_axis=1, tiled=True
    )

    grad_cols = cols(cotangent)
    p_col, d_values = attention_forward(
        cols(q_col), cols(k_col), grad_cols, table, levels(row_positions), True
    )
    d_rows = lax.all_to_all(
        d_values.reshape(images, col_count, G, D), "grid", split_axis=2, concat_axis=1, tiled=True
    )

    value_cols = jnp.dot(
        cols(col_out).reshape(-1, D), whole_weight, preferred_element_type=jnp.float32
    ).astype(jnp.bfloat16).reshape(images * col_count, G, D)
    attended, col_table = attention_backward(
        p_col, value_cols, grad_cols, fold_index(row_positions), True
    )
    attended = attended.reshape(images, col_count, G, D).transpose(0, 2, 1, 3)

    d_flat = lax.dot_general(
        d_rows.transpose(0, 2, 1, 3).reshape(-1, D), whole_weight, NT,
        preferred_element_type=jnp.float32,
    )
    d_row_out = d_flat.astype(jnp.bfloat16).reshape(images * row_count, G, D)
    (row_table,) = attention_backward(
        p_row, rows(v_row), d_row_out, fold_index(col_positions), False
    )

    batch_size = lax.axis_size("dp") * images
    table_grad = (row_table + col_table)[:, :NOFF] / (batch_size * G)
    pre_grad = table_grad * 16.0 * squashed * (1.0 - squashed)
    grad_out = lax.dot_general(
        hidden_units, pre_grad, (((0,), (1,)), ((), ())), precision=PRECISE
    )
    back_units = lax.dot_general(pre_grad, all_out, (((0,), (1,)), ((), ())), precision=PRECISE)
    unit_grad = jnp.where(pre_act > 0, back_units, 0.0)
    grad_in = jnp.sum(unit_grad * coords[:, None], axis=0)
    grad_bias = jnp.sum(unit_grad, axis=0)
    grad_mlp_out, grad_mlp_in, grad_mlp_bias = reduce_units(grad_out, grad_in, grad_bias)
    return (attended, grad_mlp_in, grad_mlp_bias, grad_mlp_out)


def solution(mesh):
    return jax.shard_map(
        shards,
        mesh=mesh,
        in_specs=(
            P("dp", "grid", None, None),
            P("dp", "grid", None, None),
            P("dp", "grid", None, None),
            P("dp", None, "grid", None),
            P("dp", None, "grid", None),
            P("dp", None, "grid", None),
            P(("dp", "grid"), None),
            P(),
            P(),
            P("grid"),
            P("grid"),
            P("grid", None),
        ),
        out_specs=(P("dp", None, "grid", None), P("grid"), P("grid"), P("grid", None)),
        check_vma=False,
    )
```

```python
import functools

import jax
import jax.numpy as jnp
from jax import lax
from jax.experimental import pallas as pl
from jax.experimental.pallas import tpu as pltpu
from jax.sharding import PartitionSpec as P


G = 96
D = 1536
NH = 48
HD = 32
HM = 512
NOFF = 191
GRID = 32
DP = 8
LANES = 128
PACK = LANES // HD
GROUPS = D // LANES
ROWS = PACK * G
MESSAGE = 6 * 3 * GROUPS
LOG2E = 1.4426950408889634
GRANT = 28 << 20

PRECISE = lax.Precision.HIGHEST
NT = (((1,), (1,)), ((), ()))
TN = (((0,), (0,)), ((), ()))
NN = (((1,), (0,)), ((), ()))

STACK = 2
UNROLL = GROUPS


def head_masks():
    lane = lax.broadcasted_iota(jnp.int32, (G, LANES), 1)
    return [(lane >= j * HD) & (lane < (j + 1) * HD) for j in range(PACK)]


def stack_heads(x, masks):
    zero = jnp.zeros_like(x)
    return jnp.concatenate([jnp.where(m, x, zero) for m in masks], axis=0)


def lane_group(g):
    return pl.ds(pl.multiple_of(g * LANES, LANES), LANES)


def head_rows(g, first):
    return pl.ds(pl.multiple_of(g * ROWS + first * G, G), STACK * G)


def softmax_rows(key, query, bias, masks):
    s = lax.dot_general(stack_heads(key, masks), query, NT, preferred_element_type=jnp.float32)
    s = s * (HD ** (-0.5) * LOG2E) + bias
    s = s.reshape(STACK, G, G)
    e = jnp.exp2(s - jnp.max(s, axis=1, keepdims=True))
    p = e * (1.0 / jnp.sum(e, axis=1, keepdims=True))
    return p.reshape(STACK * G, G).astype(jnp.bfloat16)


def pick(row, index):
    return jnp.take_along_axis(row, index, axis=1, mode="promise_in_bounds")


def forward_kernel(
    q_ref, k_ref, x_ref, table_ref, level_ref, p_ref, o_ref, bias_ref, sent_ref, *, transpose
):
    masks = head_masks()

    @pl.when(pl.program_id(0) == 0)
    def _():
        level = level_ref[...]
        index = jnp.bitwise_and(level, LANES - 1)
        high = level >= LANES

        def spread(block, carry):
            table = table_ref[pl.ds(pl.multiple_of(block * 8, 8), 8), :]
            for j in range(8):
                low = jnp.broadcast_to(table[j:j + 1, :LANES], (G, LANES))
                up = jnp.broadcast_to(table[j:j + 1, LANES:], (G, LANES))
                rows = pl.ds(pl.multiple_of((block * 8 + j) * G, G), G)
                bias_ref[rows, :] = jnp.where(high, pick(up, index), pick(low, index))
            return carry

        lax.fori_loop(0, NH // 8, spread, 0)

    def body(g, carry):
        sl = lane_group(g)
        query, key, x = q_ref[0, :, sl], k_ref[0, :, sl], x_ref[0, :, sl]
        o = None
        for first in range(0, PACK, STACK):
            own = masks[first:first + STACK]
            rows = head_rows(g, first)
            p = softmax_rows(key, query, bias_ref[rows, :G], own)
            p_ref[0, rows, :] = p
            if transpose:
                r = lax.dot_general(p, x, NN, preferred_element_type=jnp.float32)
                for j in range(STACK):
                    o = jnp.where(own[j], r[j * G:(j + 1) * G], 0.0 if o is None else o)
            else:
                r = lax.dot_general(
                    p, stack_heads(x, own), TN, preferred_element_type=jnp.float32
                )
                o = r if o is None else o + r
        if sent_ref is None:
            o_ref[0, :, sl] = o.astype(jnp.bfloat16)
        else:
            first = pl.program_id(0) * GROUPS + g
            sent_ref[pl.ds(first, G, stride=MESSAGE // 3), :] = o
        return carry

    lax.fori_loop(0, GROUPS, body, 0, unroll=UNROLL)

    if sent_ref is not None:

        @pl.when(pl.program_id(0) == pl.num_programs(0) - 1)
        def _():
            def flush(j, carry):
                rows = pl.ds(pl.multiple_of(j * 4 * MESSAGE, 4 * MESSAGE), 4 * MESSAGE)
                out = pl.ds(pl.multiple_of(j * 4, 4), 4)
                o_ref[out] = sent_ref[rows, :].astype(jnp.bfloat16).reshape(4, MESSAGE, LANES)
                return carry

            lax.fori_loop(0, GRID // 4, flush, 0)


def backward_kernel(p_ref, v_ref, g_ref, index_ref, *outs, attend):
    fold_ref, sum_ref = outs[-2:]
    masks = head_masks()

    @pl.when(pl.program_id(0) == 0)
    def _():
        sum_ref[...] = jnp.zeros_like(sum_ref)

    def body(g, carry):
        sl = lane_group(g)
        value, grad = v_ref[0, :, sl], g_ref[0, :, sl]
        o = None
        for first in range(0, PACK, STACK):
            rows = head_rows(g, first)
            vs = stack_heads(value, masks[first:first + STACK])
            p = p_ref[0, rows, :]
            if attend:
                r = lax.dot_general(p, vs, TN, preferred_element_type=jnp.float32)
                o = r if o is None else o + r
            dp = lax.dot_general(vs, grad, NT, preferred_element_type=jnp.float32)
            dp = dp.reshape(STACK, G, G)
            pf = p.astype(jnp.float32).reshape(STACK, G, G)
            ds = pf * (dp - jnp.sum(pf * dp, axis=1, keepdims=True))
            sum_ref[rows, :G] += ds.reshape(STACK * G, G)
        if attend:
            outs[0][0, :, sl] = o.astype(jnp.bfloat16)
        return carry

    lax.fori_loop(0, GROUPS, body, 0, unroll=UNROLL)

    @pl.when(pl.program_id(0) == pl.num_programs(0) - 1)
    def _():
        low, high = index_ref[:, :LANES], index_ref[:, LANES:]

        def gather(block, carry):
            lows, highs = [], []
            for j in range(8):
                own = sum_ref[pl.ds(pl.multiple_of((block * 8 + j) * G, G), G), :]
                lows.append(jnp.sum(pick(own, low), axis=0, keepdims=True))
                highs.append(jnp.sum(pick(own, high), axis=0, keepdims=True))
            rows = pl.ds(pl.multiple_of(block * 8, 8), 8)
            fold_ref[rows, :LANES] = jnp.concatenate(lows, axis=0)
            fold_ref[rows, LANES:] = jnp.concatenate(highs, axis=0)
            return carry

        lax.fori_loop(0, NH // 8, gather, 0)


BLOCK = (1, G, D)
PSHAPE = (1, NH * G, G)


def each(shape):
    return pl.BlockSpec(shape, lambda i: (i, 0, 0))


def whole(shape):
    return pl.BlockSpec(shape, lambda i: (0,) * len(shape))


def attention_forward(q, k, x, table, level, transpose):
    n = q.shape[0]
    scratch = [pltpu.VMEM((NH * G, LANES), jnp.float32)]
    kernel = functools.partial(forward_kernel, transpose=transpose)
    if transpose:
        kernel = functools.partial(kernel, sent_ref=None)
        spec, shape = each(BLOCK), (n, G, D)
    else:
        scratch.append(pltpu.VMEM((GRID * MESSAGE, LANES), jnp.float32))
        spec, shape = whole((GRID, MESSAGE, LANES)), (GRID, MESSAGE, LANES)
    return pl.pallas_call(
        kernel,
        grid=(n,),
        compiler_params=pltpu.CompilerParams(vmem_limit_bytes=GRANT),
        in_specs=[each(BLOCK)] * 3 + [whole((NH, 2 * LANES)), whole((G, LANES))],
        out_specs=[each(PSHAPE), spec],
        out_shape=[
            jax.ShapeDtypeStruct((n, NH * G, G), jnp.bfloat16),
            jax.ShapeDtypeStruct(shape, jnp.bfloat16),
        ],
        scratch_shapes=scratch,
        cost_estimate=pl.CostEstimate(
            flops=n * NH * 16 * G * G * LANES, transcendentals=n * NH * G * G, bytes_accessed=20_000_000
        ),
    )(q, k, x, table, level)


def attention_backward(p, v, g, index, attend):
    n = p.shape[0]
    specs = [each(BLOCK)] if attend else []
    shapes = [jax.ShapeDtypeStruct((n, G, D), jnp.bfloat16)] if attend else []
    return pl.pallas_call(
        functools.partial(backward_kernel, attend=attend),
        grid=(n,),
        compiler_params=pltpu.CompilerParams(vmem_limit_bytes=GRANT),
        in_specs=[each(PSHAPE), each(BLOCK), each(BLOCK), whole((G, 2 * LANES))],
        out_specs=specs + [whole((NH, 2 * LANES))],
        out_shape=shapes + [jax.ShapeDtypeStruct((NH, 2 * LANES), jnp.float32)],
        scratch_shapes=[pltpu.VMEM((NH * G, LANES), jnp.float32)],
        cost_estimate=pl.CostEstimate(
            flops=n * NH * 16 * G * G * LANES, transcendentals=0, bytes_accessed=20_000_000
        ),
    )(p, v, g, index)


def levels(positions):
    level = positions[None, :] - positions[:, None] + (G - 1)
    return jnp.pad(level, ((0, 0), (0, LANES - G)))


def fold_index(positions):
    level = positions[None, :] - positions[:, None] + (G - 1)
    hit = level[:, :, None] == jnp.arange(2 * LANES)[None, None, :]
    spot = jnp.arange(G, dtype=jnp.int32)[None, :, None] - (LANES - 1)
    return jnp.sum(jnp.where(hit, spot, 0), axis=1) + (LANES - 1)


def assemble_kernel(start_ref, *refs):
    out_ref = refs[-1]
    for j in range(DP):
        first = pl.multiple_of(start_ref[j], D // DP)
        out_ref[pl.ds(first, D // DP), :] = refs[j][...]


def assemble(parts, starts):
    return pl.pallas_call(
        assemble_kernel,
        in_specs=[pl.BlockSpec(memory_space=pltpu.SMEM)] + [pl.BlockSpec(memory_space=pltpu.VMEM)] * DP,
        out_specs=pl.BlockSpec(memory_space=pltpu.VMEM),
        out_shape=jax.ShapeDtypeStruct((D, D), jnp.bfloat16),
        compiler_params=pltpu.CompilerParams(vmem_limit_bytes=GRANT),
        cost_estimate=pl.CostEstimate(flops=0, transcendentals=0, bytes_accessed=2 * D * D * 2),
    )(starts, *parts)


def offset_coords():
    delta = jnp.arange(NOFF, dtype=jnp.float32) - (G - 1)
    scaled = delta * (8.0 / (G - 1))
    return jnp.sign(scaled) * jnp.log2(jnp.abs(scaled) + 1.0) / 3.0


UNITS = HM // GRID
HALF = UNITS // 2
WIDE = LANES // 2


def column(row):
    n = row.shape[1]
    i = lax.broadcasted_iota(jnp.int32, (n, n), 0)
    j = lax.broadcasted_iota(jnp.int32, (n, n), 1)
    return jnp.sum(jnp.where(i == j, jnp.broadcast_to(row, (n, n)), 0.0), axis=1, keepdims=True)


def pack_kernel(in_ref, bias_ref, out_ref, tile_ref):
    rest = jnp.zeros((UNITS, WIDE - NH - 2), jnp.float32)
    rows = jnp.concatenate([out_ref[...], column(in_ref[...]), column(bias_ref[...]), rest], axis=1)
    tile = jnp.concatenate([rows[:HALF], rows[HALF:]], axis=1)
    tile_ref[...] = jnp.broadcast_to(tile[None], (GRID, HALF, LANES))


def halves(tiles):
    return jnp.concatenate([tiles[:, :WIDE], tiles[:, WIDE:]], axis=0)


def table_kernel(unit_ref, coord_ref, table_ref, squashed_ref):
    units = halves(unit_ref[...])
    pre_act = units[:, NH:NH + 1] * coord_ref[...] + units[:, NH + 1:NH + 2]
    hidden = jnp.maximum(pre_act, 0.0)
    pre = lax.dot_general(
        units[:, :NH], hidden, TN, precision=PRECISE, preferred_element_type=jnp.float32
    )
    squashed = 1.0 / (1.0 + jnp.exp(-pre))
    squashed_ref[...] = squashed
    table_ref[...] = squashed * (16.0 * LOG2E)


def grad_kernel(unit_ref, coord_ref, squashed_ref, row_ref, col_ref, out_ref, *, scale):
    units = halves(unit_ref[...])
    coords = coord_ref[...]
    pre_act = units[:, NH:NH + 1] * coords + units[:, NH + 1:NH + 2]
    hidden = jnp.maximum(pre_act, 0.0)
    squashed = squashed_ref[...]
    pre_grad = (row_ref[...] + col_ref[...]) * scale * 16.0 * squashed * (1.0 - squashed)
    grad_out = lax.dot_general(
        hidden, pre_grad, NT, precision=PRECISE, preferred_element_type=jnp.float32
    )
    back = lax.dot_general(
        units[:, :NH], pre_grad, NN, precision=PRECISE, preferred_element_type=jnp.float32
    )
    unit_grad = jnp.where(pre_act > 0, back, 0.0)
    grad_in = jnp.sum(unit_grad * coords, axis=1, keepdims=True)
    grad_bias = jnp.sum(unit_grad, axis=1, keepdims=True)
    rest = jnp.zeros((HM, WIDE - NH - 2), jnp.float32)
    rows = jnp.concatenate([grad_out, grad_in, grad_bias, rest], axis=1)
    out_ref[...] = jnp.concatenate([rows[:HM // 2], rows[HM // 2:]], axis=1)


def unpack_kernel(got_ref, out_ref, in_ref, bias_ref):
    units = halves(jnp.sum(got_ref[...], axis=0))
    out_ref[...] = units[:, :NH]
    i = lax.broadcasted_iota(jnp.int32, (UNITS, UNITS), 0)
    j = lax.broadcasted_iota(jnp.int32, (UNITS, UNITS), 1)
    for lane, ref in ((NH, in_ref), (NH + 1, bias_ref)):
        spread = jnp.broadcast_to(units[:, lane:lane + 1], (UNITS, UNITS))
        ref[...] = jnp.sum(jnp.where(i == j, spread, 0.0), axis=0, keepdims=True)


def gather_units(mlp_in, mlp_bias, mlp_out):
    tiles = pl.pallas_call(
        pack_kernel, out_shape=jax.ShapeDtypeStruct((GRID, HALF, LANES), jnp.float32)
    )(mlp_in[None], mlp_bias[None], mlp_out)
    got = lax.all_to_all(tiles, "grid", 0, 0, tiled=True)
    return got.reshape(HM // 2, LANES)


def bias_tables(units, coords):
    shape = jax.ShapeDtypeStruct((NH, 2 * LANES), jnp.float32)
    return pl.pallas_call(table_kernel, out_shape=[shape, shape])(units, coords)


def unit_grads(units, coords, squashed, row_table, col_table, scale):
    return pl.pallas_call(
        functools.partial(grad_kernel, scale=scale),
        out_shape=jax.ShapeDtypeStruct((HM // 2, LANES), jnp.float32),
    )(units, coords, squashed, row_table, col_table)


def reduce_units(grads):
    got = lax.all_to_all(grads.reshape(GRID, HALF, LANES), "grid", 0, 0, tiled=True)
    own = jnp.broadcast_to(jnp.sum(got, axis=0)[None], (DP, HALF, LANES))
    got = lax.all_to_all(own, "dp", 0, 0, tiled=True)
    row = jax.ShapeDtypeStruct((1, UNITS), jnp.float32)
    grad_out, grad_in, grad_bias = pl.pallas_call(
        unpack_kernel, out_shape=[jax.ShapeDtypeStruct((UNITS, NH), jnp.float32), row, row]
    )(got)
    return grad_out, grad_in[0], grad_bias[0]


def along_x(step, swap):
    return [(i, ((i // 2 + step) % 4) * 2 + ((i % 2) ^ swap)) for i in range(DP)]


def order_kernel(swap_ref, mine_ref, other_ref, out_ref):
    half = mine_ref.shape[0]
    for first, (a_ref, b_ref) in ((0, (mine_ref, other_ref)), (1, (other_ref, mine_ref))):

        @pl.when(swap_ref[0] == first)
        def _():
            out_ref[:half] = a_ref[...]
            out_ref[half:] = b_ref[...]


def in_order(mine, other, swap):
    rows = mine.shape[0]
    return pl.pallas_call(
        order_kernel,
        in_specs=[pl.BlockSpec(memory_space=pltpu.SMEM)] + [pl.BlockSpec(memory_space=pltpu.VMEM)] * 2,
        out_specs=pl.BlockSpec(memory_space=pltpu.VMEM),
        out_shape=jax.ShapeDtypeStruct((2 * rows, D), jnp.bfloat16),
        compiler_params=pltpu.CompilerParams(vmem_limit_bytes=8 << 20),
        cost_estimate=pl.CostEstimate(flops=0, transcendentals=0, bytes_accessed=8 * rows * D),
    )(swap[None].astype(jnp.int32), mine, other)


def fetch_weight(w_value):
    here = lax.axis_index("grid")
    part = w_value
    for bit in range(5):
        other = lax.ppermute(part, "grid", [(g, g ^ (1 << bit)) for g in range(GRID)])
        part = in_order(part, other, (here >> bit) & 1)
    mine = [part]
    for step in (1, 2, 3):
        mine.append(lax.ppermute(part, "dp", along_x(step, 0)))
    other = []
    for step in range(4):
        other.append(lax.ppermute(mine[step], "dp", along_x(0, 1)))
    here = lax.axis_index("dp")
    x, core = here // 2, here % 2
    order = (x - jnp.arange(4)) % 4 * 2
    starts = jnp.concatenate([order + core, order + (1 - core)]) * (D // DP)
    return assemble(mine + other, starts.astype(jnp.int32))


def shards(
    q_row, k_row, v_row, q_col, k_col, cotangent, w_value,
    row_positions, col_positions, mlp_in, mlp_bias, mlp_out,
):
    images = q_row.shape[0]
    row_count = q_row.shape[1]
    col_count = q_col.shape[2]
    units = gather_units(mlp_in, mlp_bias, mlp_out)
    coords = jnp.pad(offset_coords(), (0, 2 * LANES - NOFF))[None]
    table, squashed = bias_tables(units, coords)
    whole_weight = fetch_weight(w_value)

    rows = lambda x: x.reshape(images * row_count, G, D)
    cols = lambda x: x.transpose(0, 2, 1, 3).reshape(images * col_count, G, D)
    p_row, row_out = attention_forward(
        rows(q_row), rows(k_row), rows(v_row), table, levels(col_positions), False
    )
    col_out = lax.all_to_all(row_out, "grid", split_axis=0, concat_axis=0, tiled=True)

    grad_cols = cols(cotangent)
    p_col, d_values = attention_forward(
        cols(q_col), cols(k_col), grad_cols, table, levels(row_positions), True
    )
    d_rows = lax.all_to_all(
        d_values.reshape(images, col_count, G, D), "grid", split_axis=2, concat_axis=1, tiled=True
    )

    col_tokens = col_out.reshape(GRID, col_count, images, row_count, D).transpose(2, 1, 0, 3, 4)
    value_cols = jnp.dot(
        col_tokens.reshape(-1, D), whole_weight, preferred_element_type=jnp.float32
    ).astype(jnp.bfloat16).reshape(images * col_count, G, D)
    attended, col_table = attention_backward(
        p_col, value_cols, grad_cols, fold_index(row_positions), True
    )
    attended = attended.reshape(images, col_count, G, D).transpose(0, 2, 1, 3)

    d_flat = lax.dot_general(
        d_rows.transpose(0, 2, 1, 3).reshape(-1, D), whole_weight, NT,
        preferred_element_type=jnp.float32,
    )
    d_row_out = d_flat.astype(jnp.bfloat16).reshape(images * row_count, G, D)
    (row_table,) = attention_backward(
        p_row, rows(v_row), d_row_out, fold_index(col_positions), False
    )

    batch_size = lax.axis_size("dp") * images
    grads = unit_grads(units, coords, squashed, row_table, col_table, 1.0 / (batch_size * G))
    grad_mlp_out, grad_mlp_in, grad_mlp_bias = reduce_units(grads)
    return (attended, grad_mlp_in, grad_mlp_bias, grad_mlp_out)


def solution(mesh):
    return jax.shard_map(
        shards,
        mesh=mesh,
        in_specs=(
            P("dp", "grid", None, None),
            P("dp", "grid", None, None),
            P("dp", "grid", None, None),
            P("dp", None, "grid", None),
            P("dp", None, "grid", None),
            P("dp", None, "grid", None),
            P(("dp", "grid"), None),
            P(),
            P(),
            P("grid"),
            P("grid"),
            P("grid", None),
        ),
        out_specs=(P("dp", None, "grid", None), P("grid"), P("grid"), P("grid", None)),
        check_vma=False,
    )
```

```python
import functools

import jax
import jax.numpy as jnp
from jax import lax
from jax.experimental import pallas as pl
from jax.experimental.pallas import tpu as pltpu
from jax.sharding import PartitionSpec as P


G = 96
D = 1536
NH = 48
HD = 32
HM = 512
NOFF = 191
GRID = 32
DP = 8
LANES = 128
PACK = LANES // HD
GROUPS = D // LANES
ROWS = PACK * G
MESSAGE = 6 * 3 * GROUPS
LOG2E = 1.4426950408889634
GRANT = 28 << 20

PRECISE = lax.Precision.HIGHEST
NT = (((1,), (1,)), ((), ()))
TN = (((0,), (0,)), ((), ()))
NN = (((1,), (0,)), ((), ()))

STACK = 2
UNROLL = GROUPS


def head_masks():
    lane = lax.broadcasted_iota(jnp.int32, (G, LANES), 1)
    return [(lane >= j * HD) & (lane < (j + 1) * HD) for j in range(PACK)]


def stack_heads(x, masks):
    zero = jnp.zeros_like(x)
    return jnp.concatenate([jnp.where(m, x, zero) for m in masks], axis=0)


def lane_group(g):
    return pl.ds(pl.multiple_of(g * LANES, LANES), LANES)


def head_rows(g, first):
    return pl.ds(pl.multiple_of(g * ROWS + first * G, G), STACK * G)


def softmax_rows(key, query, bias, masks):
    s = lax.dot_general(stack_heads(key, masks), query, NT, preferred_element_type=jnp.float32)
    s = s * (HD ** (-0.5) * LOG2E) + bias
    s = s.reshape(STACK, G, G)
    e = jnp.exp2(s - jnp.max(s, axis=1, keepdims=True))
    p = e * (1.0 / jnp.sum(e, axis=1, keepdims=True))
    return p.reshape(STACK * G, G).astype(jnp.bfloat16)


def pick(row, index):
    return jnp.take_along_axis(row, index, axis=1, mode="promise_in_bounds")


def forward_kernel(
    q_ref, k_ref, x_ref, table_ref, level_ref, p_ref, o_ref, bias_ref, sent_ref, *, transpose
):
    masks = head_masks()

    @pl.when(pl.program_id(0) == 0)
    def _():
        level = level_ref[...]
        index = jnp.bitwise_and(level, LANES - 1)
        high = level >= LANES

        def spread(block, carry):
            table = table_ref[pl.ds(pl.multiple_of(block * 8, 8), 8), :]
            for j in range(8):
                low = jnp.broadcast_to(table[j:j + 1, :LANES], (G, LANES))
                up = jnp.broadcast_to(table[j:j + 1, LANES:], (G, LANES))
                rows = pl.ds(pl.multiple_of((block * 8 + j) * G, G), G)
                bias_ref[rows, :] = jnp.where(high, pick(up, index), pick(low, index))
            return carry

        lax.fori_loop(0, NH // 8, spread, 0)

    def body(g, carry):
        sl = lane_group(g)
        query, key, x = q_ref[0, :, sl], k_ref[0, :, sl], x_ref[0, :, sl]
        o = None
        for first in range(0, PACK, STACK):
            own = masks[first:first + STACK]
            rows = head_rows(g, first)
            p = softmax_rows(key, query, bias_ref[rows, :G], own)
            p_ref[0, rows, :] = p
            if transpose:
                r = lax.dot_general(p, x, NN, preferred_element_type=jnp.float32)
                for j in range(STACK):
                    o = jnp.where(own[j], r[j * G:(j + 1) * G], 0.0 if o is None else o)
            else:
                r = lax.dot_general(
                    p, stack_heads(x, own), TN, preferred_element_type=jnp.float32
                )
                o = r if o is None else o + r
        if sent_ref is None:
            o_ref[0, :, sl] = o.astype(jnp.bfloat16)
        else:
            first = pl.program_id(0) * GROUPS + g
            sent_ref[pl.ds(first, G, stride=MESSAGE // 3), :] = o
        return carry

    lax.fori_loop(0, GROUPS, body, 0, unroll=UNROLL)

    if sent_ref is not None:

        @pl.when(pl.program_id(0) == pl.num_programs(0) - 1)
        def _():
            def flush(j, carry):
                rows = pl.ds(pl.multiple_of(j * 4 * MESSAGE, 4 * MESSAGE), 4 * MESSAGE)
                out = pl.ds(pl.multiple_of(j * 4, 4), 4)
                o_ref[out] = sent_ref[rows, :].astype(jnp.bfloat16).reshape(4, MESSAGE, LANES)
                return carry

            lax.fori_loop(0, GRID // 4, flush, 0)


def backward_kernel(p_ref, v_ref, g_ref, index_ref, *outs, attend):
    fold_ref, sum_ref = outs[-2:]
    masks = head_masks()

    @pl.when(pl.program_id(0) == 0)
    def _():
        sum_ref[...] = jnp.zeros_like(sum_ref)

    def body(g, carry):
        sl = lane_group(g)
        value, grad = v_ref[0, :, sl], g_ref[0, :, sl]
        o = None
        for first in range(0, PACK, STACK):
            rows = head_rows(g, first)
            vs = stack_heads(value, masks[first:first + STACK])
            p = p_ref[0, rows, :]
            if attend:
                r = lax.dot_general(p, vs, TN, preferred_element_type=jnp.float32)
                o = r if o is None else o + r
            dp = lax.dot_general(vs, grad, NT, preferred_element_type=jnp.float32)
            dp = dp.reshape(STACK, G, G)
            pf = p.astype(jnp.float32).reshape(STACK, G, G)
            ds = pf * (dp - jnp.sum(pf * dp, axis=1, keepdims=True))
            sum_ref[rows, :G] += ds.reshape(STACK * G, G)
        if attend:
            outs[0][0, :, sl] = o.astype(jnp.bfloat16)
        return carry

    lax.fori_loop(0, GROUPS, body, 0, unroll=UNROLL)

    @pl.when(pl.program_id(0) == pl.num_programs(0) - 1)
    def _():
        lane = lax.broadcasted_iota(jnp.int32, (G, LANES), 1)
        spot = lax.broadcasted_iota(jnp.int32, (G, LANES), 0)
        position = jnp.broadcast_to(index_ref[...], (G, LANES))
        inverse = jnp.sum(jnp.where(position == lane, spot, 0), axis=0, keepdims=True)
        inverse = jnp.broadcast_to(inverse, (G, LANES))

        def at(offset):
            place = offset + position - (G - 1)
            found = pick(inverse, jnp.bitwise_and(place, LANES - 1))
            return jnp.where((place >= 0) & (place < G), found, LANES - 1)

        low, high = at(lane), at(lane + LANES)

        def gather(block, carry):
            lows, highs = [], []
            for j in range(8):
                own = sum_ref[pl.ds(pl.multiple_of((block * 8 + j) * G, G), G), :]
                lows.append(jnp.sum(pick(own, low), axis=0, keepdims=True))
                highs.append(jnp.sum(pick(own, high), axis=0, keepdims=True))
            rows = pl.ds(pl.multiple_of(block * 8, 8), 8)
            fold_ref[rows, :LANES] = jnp.concatenate(lows, axis=0)
            fold_ref[rows, LANES:] = jnp.concatenate(highs, axis=0)
            return carry

        lax.fori_loop(0, NH // 8, gather, 0)


BLOCK = (1, G, D)
PSHAPE = (1, NH * G, G)


def each(shape):
    return pl.BlockSpec(shape, lambda i: (i, 0, 0))


def whole(shape):
    return pl.BlockSpec(shape, lambda i: (0,) * len(shape))


def attention_forward(q, k, x, table, level, transpose):
    n = q.shape[0]
    scratch = [pltpu.VMEM((NH * G, LANES), jnp.float32)]
    kernel = functools.partial(forward_kernel, transpose=transpose)
    if transpose:
        kernel = functools.partial(kernel, sent_ref=None)
        spec, shape = each(BLOCK), (n, G, D)
    else:
        scratch.append(pltpu.VMEM((GRID * MESSAGE, LANES), jnp.float32))
        spec, shape = whole((GRID, MESSAGE, LANES)), (GRID, MESSAGE, LANES)
    return pl.pallas_call(
        kernel,
        grid=(n,),
        in_specs=[each(BLOCK)] * 3 + [whole((NH, 2 * LANES)), whole((G, LANES))],
        out_specs=[each(PSHAPE), spec],
        out_shape=[
            jax.ShapeDtypeStruct((n, NH * G, G), jnp.bfloat16),
            jax.ShapeDtypeStruct(shape, jnp.bfloat16),
        ],
        scratch_shapes=scratch,
        cost_estimate=pl.CostEstimate(
            flops=n * NH * 16 * G * G * LANES, transcendentals=n * NH * G * G, bytes_accessed=20_000_000
        ),
    )(q, k, x, table, level)


def attention_backward(p, v, g, index, attend):
    n = p.shape[0]
    specs = [each(BLOCK)] if attend else []
    shapes = [jax.ShapeDtypeStruct((n, G, D), jnp.bfloat16)] if attend else []
    return pl.pallas_call(
        functools.partial(backward_kernel, attend=attend),
        grid=(n,),
        compiler_params=pltpu.CompilerParams(vmem_limit_bytes=GRANT),
        in_specs=[each(PSHAPE), each(BLOCK), each(BLOCK), whole((G, 1))],
        out_specs=specs + [whole((NH, 2 * LANES))],
        out_shape=shapes + [jax.ShapeDtypeStruct((NH, 2 * LANES), jnp.float32)],
        scratch_shapes=[pltpu.VMEM((NH * G, LANES), jnp.float32)],
        cost_estimate=pl.CostEstimate(
            flops=n * NH * 16 * G * G * LANES, transcendentals=0, bytes_accessed=20_000_000
        ),
    )(p, v, g, index)


def levels(positions):
    level = positions[None, :] - positions[:, None] + (G - 1)
    return jnp.pad(level, ((0, 0), (0, LANES - G)))


def assemble_kernel(start_ref, *refs):
    out_ref = refs[-1]
    for j in range(DP):
        first = pl.multiple_of(start_ref[j], D // DP)
        out_ref[pl.ds(first, D // DP), :] = refs[j][...]


def assemble(parts, starts):
    return pl.pallas_call(
        assemble_kernel,
        in_specs=[pl.BlockSpec(memory_space=pltpu.SMEM)] + [pl.BlockSpec(memory_space=pltpu.VMEM)] * DP,
        out_specs=pl.BlockSpec(memory_space=pltpu.VMEM),
        out_shape=jax.ShapeDtypeStruct((D, D), jnp.bfloat16),
        compiler_params=pltpu.CompilerParams(vmem_limit_bytes=GRANT),
        cost_estimate=pl.CostEstimate(flops=0, transcendentals=0, bytes_accessed=2 * D * D * 2),
    )(starts, *parts)


def offset_coords():
    delta = jnp.arange(NOFF, dtype=jnp.float32) - (G - 1)
    scaled = delta * (8.0 / (G - 1))
    return jnp.sign(scaled) * jnp.log2(jnp.abs(scaled) + 1.0) / 3.0


UNITS = HM // GRID
HALF = UNITS // 2
WIDE = LANES // 2


def column(row):
    n = row.shape[1]
    i = lax.broadcasted_iota(jnp.int32, (n, n), 0)
    j = lax.broadcasted_iota(jnp.int32, (n, n), 1)
    return jnp.sum(jnp.where(i == j, jnp.broadcast_to(row, (n, n)), 0.0), axis=1, keepdims=True)


def pack_kernel(in_ref, bias_ref, out_ref, tile_ref):
    rest = jnp.zeros((UNITS, WIDE - NH - 2), jnp.float32)
    rows = jnp.concatenate([out_ref[...], column(in_ref[...]), column(bias_ref[...]), rest], axis=1)
    tile = jnp.concatenate([rows[:HALF], rows[HALF:]], axis=1)
    tile_ref[...] = jnp.broadcast_to(tile[None], (GRID, HALF, LANES))


def halves(tiles):
    return jnp.concatenate([tiles[:, :WIDE], tiles[:, WIDE:]], axis=0)


def table_kernel(unit_ref, coord_ref, table_ref, squashed_ref):
    units = halves(unit_ref[...])
    pre_act = units[:, NH:NH + 1] * coord_ref[...] + units[:, NH + 1:NH + 2]
    hidden = jnp.maximum(pre_act, 0.0)
    pre = lax.dot_general(
        units[:, :NH], hidden, TN, precision=PRECISE, preferred_element_type=jnp.float32
    )
    squashed = 1.0 / (1.0 + jnp.exp(-pre))
    squashed_ref[...] = squashed
    table_ref[...] = squashed * (16.0 * LOG2E)


def grad_kernel(unit_ref, coord_ref, squashed_ref, row_ref, col_ref, out_ref, *, scale):
    units = halves(unit_ref[...])
    coords = coord_ref[...]
    pre_act = units[:, NH:NH + 1] * coords + units[:, NH + 1:NH + 2]
    hidden = jnp.maximum(pre_act, 0.0)
    squashed = squashed_ref[...]
    pre_grad = (row_ref[...] + col_ref[...]) * scale * 16.0 * squashed * (1.0 - squashed)
    grad_out = lax.dot_general(
        hidden, pre_grad, NT, precision=PRECISE, preferred_element_type=jnp.float32
    )
    back = lax.dot_general(
        units[:, :NH], pre_grad, NN, precision=PRECISE, preferred_element_type=jnp.float32
    )
    unit_grad = jnp.where(pre_act > 0, back, 0.0)
    grad_in = jnp.sum(unit_grad * coords, axis=1, keepdims=True)
    grad_bias = jnp.sum(unit_grad, axis=1, keepdims=True)
    rest = jnp.zeros((HM, WIDE - NH - 2), jnp.float32)
    rows = jnp.concatenate([grad_out, grad_in, grad_bias, rest], axis=1)
    out_ref[...] = jnp.concatenate([rows[:HM // 2], rows[HM // 2:]], axis=1)


def unpack_kernel(got_ref, out_ref, in_ref, bias_ref):
    units = halves(jnp.sum(got_ref[...], axis=0))
    out_ref[...] = units[:, :NH]
    i = lax.broadcasted_iota(jnp.int32, (UNITS, UNITS), 0)
    j = lax.broadcasted_iota(jnp.int32, (UNITS, UNITS), 1)
    for lane, ref in ((NH, in_ref), (NH + 1, bias_ref)):
        spread = jnp.broadcast_to(units[:, lane:lane + 1], (UNITS, UNITS))
        ref[...] = jnp.sum(jnp.where(i == j, spread, 0.0), axis=0, keepdims=True)


def gather_units(mlp_in, mlp_bias, mlp_out):
    tiles = pl.pallas_call(
        pack_kernel, out_shape=jax.ShapeDtypeStruct((GRID, HALF, LANES), jnp.float32)
    )(mlp_in[None], mlp_bias[None], mlp_out)
    got = lax.all_to_all(tiles, "grid", 0, 0, tiled=True)
    return got.reshape(HM // 2, LANES)


def bias_tables(units, coords):
    shape = jax.ShapeDtypeStruct((NH, 2 * LANES), jnp.float32)
    return pl.pallas_call(table_kernel, out_shape=[shape, shape])(units, coords)


def unit_grads(units, coords, squashed, row_table, col_table, scale):
    return pl.pallas_call(
        functools.partial(grad_kernel, scale=scale),
        out_shape=jax.ShapeDtypeStruct((HM // 2, LANES), jnp.float32),
    )(units, coords, squashed, row_table, col_table)


def reduce_units(grads):
    got = lax.all_to_all(grads.reshape(GRID, HALF, LANES), "grid", 0, 0, tiled=True)
    own = jnp.broadcast_to(jnp.sum(got, axis=0)[None], (DP, HALF, LANES))
    got = lax.all_to_all(own, "dp", 0, 0, tiled=True)
    row = jax.ShapeDtypeStruct((1, UNITS), jnp.float32)
    grad_out, grad_in, grad_bias = pl.pallas_call(
        unpack_kernel, out_shape=[jax.ShapeDtypeStruct((UNITS, NH), jnp.float32), row, row]
    )(got)
    return grad_out, grad_in[0], grad_bias[0]


def along_x(step, swap):
    return [(i, ((i // 2 + step) % 4) * 2 + ((i % 2) ^ swap)) for i in range(DP)]


def order_kernel(swap_ref, mine_ref, other_ref, out_ref):
    half = mine_ref.shape[0]
    for first, (a_ref, b_ref) in ((0, (mine_ref, other_ref)), (1, (other_ref, mine_ref))):

        @pl.when(swap_ref[0] == first)
        def _():
            out_ref[:half] = a_ref[...]
            out_ref[half:] = b_ref[...]


def in_order(mine, other, swap):
    rows = mine.shape[0]
    return pl.pallas_call(
        order_kernel,
        in_specs=[pl.BlockSpec(memory_space=pltpu.SMEM)] + [pl.BlockSpec(memory_space=pltpu.VMEM)] * 2,
        out_specs=pl.BlockSpec(memory_space=pltpu.VMEM),
        out_shape=jax.ShapeDtypeStruct((2 * rows, D), jnp.bfloat16),
        compiler_params=pltpu.CompilerParams(vmem_limit_bytes=8 << 20),
        cost_estimate=pl.CostEstimate(flops=0, transcendentals=0, bytes_accessed=8 * rows * D),
    )(swap[None].astype(jnp.int32), mine, other)


def fetch_weight(w_value):
    here = lax.axis_index("grid")
    part = w_value
    for bit in range(5):
        other = lax.ppermute(part, "grid", [(g, g ^ (1 << bit)) for g in range(GRID)])
        part = in_order(part, other, (here >> bit) & 1)
    mine = [part]
    for step in (1, 2, 3):
        mine.append(lax.ppermute(part, "dp", along_x(step, 0)))
    other = []
    for step in range(4):
        other.append(lax.ppermute(mine[step], "dp", along_x(0, 1)))
    here = lax.axis_index("dp")
    x, core = here // 2, here % 2
    order = (x - jnp.arange(4)) % 4 * 2
    starts = jnp.concatenate([order + core, order + (1 - core)]) * (D // DP)
    return assemble(mine + other, starts.astype(jnp.int32))


def shards(
    q_row, k_row, v_row, q_col, k_col, cotangent, w_value,
    row_positions, col_positions, mlp_in, mlp_bias, mlp_out,
):
    images = q_row.shape[0]
    row_count = q_row.shape[1]
    col_count = q_col.shape[2]
    units = gather_units(mlp_in, mlp_bias, mlp_out)
    coords = jnp.pad(offset_coords(), (0, 2 * LANES - NOFF))[None]
    table, squashed = bias_tables(units, coords)
    whole_weight = fetch_weight(w_value)

    rows = lambda x: x.reshape(images * row_count, G, D)
    cols = lambda x: x.transpose(0, 2, 1, 3).reshape(images * col_count, G, D)
    p_row, row_out = attention_forward(
        rows(q_row), rows(k_row), rows(v_row), table, levels(col_positions), False
    )
    col_out = lax.all_to_all(row_out, "grid", split_axis=0, concat_axis=0, tiled=True)

    grad_cols = cols(cotangent)
    p_col, d_values = attention_forward(
        cols(q_col), cols(k_col), grad_cols, table, levels(row_positions), True
    )
    d_values = d_values.reshape(images, col_count, G, D)
    d_rows = lax.all_to_all(d_values, "grid", split_axis=2, concat_axis=1, tiled=True)

    col_tokens = col_out.reshape(GRID, col_count, images, row_count, D).transpose(2, 1, 0, 3, 4)
    col_tokens = col_tokens.reshape(-1, D)
    value_cols = jnp.dot(
        col_tokens, whole_weight, preferred_element_type=jnp.float32
    ).astype(jnp.bfloat16).reshape(images * col_count, G, D)
    attended, col_table = attention_backward(
        p_col, value_cols, grad_cols, row_positions[:, None], True
    )
    attended = attended.reshape(images, col_count, G, D).transpose(0, 2, 1, 3)

    d_flat = lax.dot_general(
        d_rows.transpose(0, 2, 1, 3).reshape(-1, D), whole_weight, NT,
        preferred_element_type=jnp.float32,
    )
    d_row_out = d_flat.astype(jnp.bfloat16).reshape(images * row_count, G, D)
    (row_table,) = attention_backward(p_row, rows(v_row), d_row_out, col_positions[:, None], False)

    batch_size = lax.axis_size("dp") * images
    grads = unit_grads(units, coords, squashed, row_table, col_table, 1.0 / (batch_size * G))
    grad_mlp_out, grad_mlp_in, grad_mlp_bias = reduce_units(grads)
    return (attended, grad_mlp_in, grad_mlp_bias, grad_mlp_out)


def solution(mesh):
    return jax.shard_map(
        shards,
        mesh=mesh,
        in_specs=(
            P("dp", "grid", None, None),
            P("dp", "grid", None, None),
            P("dp", "grid", None, None),
            P("dp", None, "grid", None),
            P("dp", None, "grid", None),
            P("dp", None, "grid", None),
            P(("dp", "grid"), None),
            P(),
            P(),
            P("grid"),
            P("grid"),
            P("grid", None),
        ),
        out_specs=(P("dp", None, "grid", None), P("grid"), P("grid"), P("grid", None)),
        check_vma=False,
    )
```

```python
import functools

import jax
import jax.numpy as jnp
from jax import lax
from jax.experimental import pallas as pl
from jax.experimental.pallas import tpu as pltpu
from jax.sharding import PartitionSpec as P


G = 96
D = 1536
NH = 48
HD = 32
HM = 512
NOFF = 191
GRID = 32
DP = 8
LANES = 128
PACK = LANES // HD
GROUPS = D // LANES
ROWS = PACK * G
MESSAGE = 6 * 3 * GROUPS
LOG2E = 1.4426950408889634
GRANT = 28 << 20

PRECISE = lax.Precision.HIGHEST
NT = (((1,), (1,)), ((), ()))
TN = (((0,), (0,)), ((), ()))
NN = (((1,), (0,)), ((), ()))

STACK = 2
UNROLL = GROUPS


def head_masks():
    lane = lax.broadcasted_iota(jnp.int32, (G, LANES), 1)
    return [(lane >= j * HD) & (lane < (j + 1) * HD) for j in range(PACK)]


def stack_heads(x, masks):
    zero = jnp.zeros_like(x)
    return jnp.concatenate([jnp.where(m, x, zero) for m in masks], axis=0)


def lane_group(g):
    return pl.ds(pl.multiple_of(g * LANES, LANES), LANES)


def head_rows(g, first):
    return pl.ds(pl.multiple_of(g * ROWS + first * G, G), STACK * G)


def softmax_rows(key, query, bias, masks):
    s = lax.dot_general(stack_heads(key, masks), query, NT, preferred_element_type=jnp.float32)
    s = s * (HD ** (-0.5) * LOG2E) + bias
    s = s.reshape(STACK, G, G)
    e = jnp.exp2(s - jnp.max(s, axis=1, keepdims=True))
    p = e * (1.0 / jnp.sum(e, axis=1, keepdims=True))
    return p.reshape(STACK * G, G).astype(jnp.bfloat16)


def both_ways(row):
    i = lax.broadcasted_iota(jnp.int32, (G, G), 0)
    j = lax.broadcasted_iota(jnp.int32, (G, G), 1)
    spread = jnp.broadcast_to(row.astype(jnp.float32), (G, G))
    down = jnp.sum(jnp.where(i == j, spread, 0.0), axis=1, keepdims=True).astype(jnp.int32)
    across = jnp.concatenate([row, jnp.zeros((1, LANES - G), jnp.int32)], axis=1)
    return jnp.broadcast_to(across, (G, LANES)), jnp.broadcast_to(down, (G, LANES))


def pick(row, index):
    return jnp.take_along_axis(row, index, axis=1, mode="promise_in_bounds")


def forward_kernel(
    q_ref, k_ref, x_ref, table_ref, pos_ref, p_ref, o_ref, bias_ref, sent_ref, *, transpose
):
    masks = head_masks()

    @pl.when(pl.program_id(0) == 0)
    def _():
        across, down = both_ways(pos_ref[...])
        level = across - down + (G - 1)
        index = jnp.bitwise_and(level, LANES - 1)
        high = level >= LANES

        def spread(block, carry):
            table = table_ref[pl.ds(pl.multiple_of(block * 8, 8), 8), :]
            for j in range(8):
                low = jnp.broadcast_to(table[j:j + 1, :LANES], (G, LANES))
                up = jnp.broadcast_to(table[j:j + 1, LANES:], (G, LANES))
                rows = pl.ds(pl.multiple_of((block * 8 + j) * G, G), G)
                bias_ref[rows, :] = jnp.where(high, pick(up, index), pick(low, index))
            return carry

        lax.fori_loop(0, NH // 8, spread, 0)

    def body(g, carry):
        sl = lane_group(g)
        query, key, x = q_ref[0, :, sl], k_ref[0, :, sl], x_ref[0, :, sl]
        o = None
        for first in range(0, PACK, STACK):
            own = masks[first:first + STACK]
            rows = head_rows(g, first)
            p = softmax_rows(key, query, bias_ref[rows, :G], own)
            p_ref[0, rows, :] = p
            if transpose:
                r = lax.dot_general(p, x, NN, preferred_element_type=jnp.float32)
                for j in range(STACK):
                    o = jnp.where(own[j], r[j * G:(j + 1) * G], 0.0 if o is None else o)
            else:
                r = lax.dot_general(
                    p, stack_heads(x, own), TN, preferred_element_type=jnp.float32
                )
                o = r if o is None else o + r
        if sent_ref is None:
            o_ref[0, :, sl] = o.astype(jnp.bfloat16)
        else:
            first = pl.program_id(0) * GROUPS + g
            sent_ref[pl.ds(first, G, stride=MESSAGE // 3), :] = o
        return carry

    lax.fori_loop(0, GROUPS, body, 0, unroll=UNROLL)

    if sent_ref is not None:

        @pl.when(pl.program_id(0) == pl.num_programs(0) - 1)
        def _():
            def flush(j, carry):
                rows = pl.ds(pl.multiple_of(j * 4 * MESSAGE, 4 * MESSAGE), 4 * MESSAGE)
                out = pl.ds(pl.multiple_of(j * 4, 4), 4)
                o_ref[out] = sent_ref[rows, :].astype(jnp.bfloat16).reshape(4, MESSAGE, LANES)
                return carry

            lax.fori_loop(0, GRID // 4, flush, 0)


def backward_kernel(p_ref, v_ref, g_ref, index_ref, *outs, attend):
    fold_ref, sum_ref = outs[-2:]
    masks = head_masks()

    @pl.when(pl.program_id(0) == 0)
    def _():
        sum_ref[...] = jnp.zeros_like(sum_ref)

    def body(g, carry):
        sl = lane_group(g)
        value, grad = v_ref[0, :, sl], g_ref[0, :, sl]
        o = None
        for first in range(0, PACK, STACK):
            rows = head_rows(g, first)
            vs = stack_heads(value, masks[first:first + STACK])
            p = p_ref[0, rows, :]
            if attend:
                r = lax.dot_general(p, vs, TN, preferred_element_type=jnp.float32)
                o = r if o is None else o + r
            dp = lax.dot_general(vs, grad, NT, preferred_element_type=jnp.float32)
            dp = dp.reshape(STACK, G, G)
            pf = p.astype(jnp.float32).reshape(STACK, G, G)
            ds = pf * (dp - jnp.sum(pf * dp, axis=1, keepdims=True))
            sum_ref[rows, :G] += ds.reshape(STACK * G, G)
        if attend:
            outs[0][0, :, sl] = o.astype(jnp.bfloat16)
        return carry

    lax.fori_loop(0, GROUPS, body, 0, unroll=UNROLL)

    @pl.when(pl.program_id(0) == pl.num_programs(0) - 1)
    def _():
        lane = lax.broadcasted_iota(jnp.int32, (G, LANES), 1)
        spot = lax.broadcasted_iota(jnp.int32, (G, LANES), 0)
        position = both_ways(index_ref[...])[1]
        inverse = jnp.sum(jnp.where(position == lane, spot, 0), axis=0, keepdims=True)
        inverse = jnp.broadcast_to(inverse, (G, LANES))

        def at(offset):
            place = offset + position - (G - 1)
            found = pick(inverse, jnp.bitwise_and(place, LANES - 1))
            return jnp.where((place >= 0) & (place < G), found, LANES - 1)

        low, high = at(lane), at(lane + LANES)

        def gather(block, carry):
            lows, highs = [], []
            for j in range(8):
                own = sum_ref[pl.ds(pl.multiple_of((block * 8 + j) * G, G), G), :]
                lows.append(jnp.sum(pick(own, low), axis=0, keepdims=True))
                highs.append(jnp.sum(pick(own, high), axis=0, keepdims=True))
            rows = pl.ds(pl.multiple_of(block * 8, 8), 8)
            fold_ref[rows, :LANES] = jnp.concatenate(lows, axis=0)
            fold_ref[rows, LANES:] = jnp.concatenate(highs, axis=0)
            return carry

        lax.fori_loop(0, NH // 8, gather, 0)


BLOCK = (1, G, D)
PSHAPE = (1, NH * G, G)


def each(shape):
    return pl.BlockSpec(shape, lambda i: (i, 0, 0))


def whole(shape):
    return pl.BlockSpec(shape, lambda i: (0,) * len(shape))


def row_forward_kernel(
    q_ref, k_ref, x_ref, unit_ref, coord_ref, pos_ref,
    p_ref, o_ref, table_ref, squashed_ref, bias_ref, sent_ref,
):
    @pl.when(pl.program_id(0) == 0)
    def _():
        table_kernel(unit_ref, coord_ref, table_ref, squashed_ref)

    forward_kernel(
        q_ref, k_ref, x_ref, table_ref, pos_ref, p_ref, o_ref, bias_ref, sent_ref, transpose=False
    )


def forward_cost(n):
    return pl.CostEstimate(
        flops=n * NH * 16 * G * G * LANES, transcendentals=n * NH * G * G, bytes_accessed=20_000_000
    )


def row_forward(q, k, v, units, coords, positions):
    n = q.shape[0]
    table = (NH, 2 * LANES)
    return pl.pallas_call(
        row_forward_kernel,
        grid=(n,),
        in_specs=[each(BLOCK)] * 3
        + [whole((HM // 2, LANES)), whole((1, 2 * LANES)), whole((1, G))],
        out_specs=[each(PSHAPE), whole((GRID, MESSAGE, LANES)), whole(table), whole(table)],
        out_shape=[
            jax.ShapeDtypeStruct((n, NH * G, G), jnp.bfloat16),
            jax.ShapeDtypeStruct((GRID, MESSAGE, LANES), jnp.bfloat16),
            jax.ShapeDtypeStruct(table, jnp.float32),
            jax.ShapeDtypeStruct(table, jnp.float32),
        ],
        scratch_shapes=[
            pltpu.VMEM((NH * G, LANES), jnp.float32),
            pltpu.VMEM((GRID * MESSAGE, LANES), jnp.float32),
        ],
        cost_estimate=forward_cost(n),
    )(q, k, v, units, coords, positions)


def col_forward(q, k, g, table, positions):
    n = q.shape[0]
    return pl.pallas_call(
        functools.partial(forward_kernel, sent_ref=None, transpose=True),
        grid=(n,),
        in_specs=[each(BLOCK)] * 3 + [whole((NH, 2 * LANES)), whole((1, G))],
        out_specs=[each(PSHAPE), each(BLOCK)],
        out_shape=[
            jax.ShapeDtypeStruct((n, NH * G, G), jnp.bfloat16),
            jax.ShapeDtypeStruct((n, G, D), jnp.bfloat16),
        ],
        scratch_shapes=[pltpu.VMEM((NH * G, LANES), jnp.float32)],
        cost_estimate=forward_cost(n),
    )(q, k, g, table, positions)


def attention_backward(p, v, g, index, attend):
    n = p.shape[0]
    specs = [each(BLOCK)] if attend else []
    shapes = [jax.ShapeDtypeStruct((n, G, D), jnp.bfloat16)] if attend else []
    return pl.pallas_call(
        functools.partial(backward_kernel, attend=attend),
        grid=(n,),
        compiler_params=pltpu.CompilerParams(vmem_limit_bytes=GRANT),
        in_specs=[each(PSHAPE), each(BLOCK), each(BLOCK), whole((1, G))],
        out_specs=specs + [whole((NH, 2 * LANES))],
        out_shape=shapes + [jax.ShapeDtypeStruct((NH, 2 * LANES), jnp.float32)],
        scratch_shapes=[pltpu.VMEM((NH * G, LANES), jnp.float32)],
        cost_estimate=pl.CostEstimate(
            flops=n * NH * 16 * G * G * LANES, transcendentals=0, bytes_accessed=20_000_000
        ),
    )(p, v, g, index)


def assemble_kernel(start_ref, *refs):
    out_ref = refs[-1]
    for j in range(DP):
        first = pl.multiple_of(start_ref[j], D // DP)
        out_ref[pl.ds(first, D // DP), :] = refs[j][...]


def assemble(parts, starts):
    return pl.pallas_call(
        assemble_kernel,
        in_specs=[pl.BlockSpec(memory_space=pltpu.SMEM)] + [pl.BlockSpec(memory_space=pltpu.VMEM)] * DP,
        out_specs=pl.BlockSpec(memory_space=pltpu.VMEM),
        out_shape=jax.ShapeDtypeStruct((D, D), jnp.bfloat16),
        compiler_params=pltpu.CompilerParams(vmem_limit_bytes=GRANT),
        cost_estimate=pl.CostEstimate(flops=0, transcendentals=0, bytes_accessed=2 * D * D * 2),
    )(starts, *parts)


def offset_coords():
    delta = jnp.arange(NOFF, dtype=jnp.float32) - (G - 1)
    scaled = delta * (8.0 / (G - 1))
    return jnp.sign(scaled) * jnp.log2(jnp.abs(scaled) + 1.0) / 3.0


UNITS = HM // GRID
HALF = UNITS // 2
WIDE = LANES // 2


def column(row):
    n = row.shape[1]
    i = lax.broadcasted_iota(jnp.int32, (n, n), 0)
    j = lax.broadcasted_iota(jnp.int32, (n, n), 1)
    return jnp.sum(jnp.where(i == j, jnp.broadcast_to(row, (n, n)), 0.0), axis=1, keepdims=True)


def pack_kernel(in_ref, bias_ref, out_ref, tile_ref):
    rest = jnp.zeros((UNITS, WIDE - NH - 2), jnp.float32)
    rows = jnp.concatenate([out_ref[...], column(in_ref[...]), column(bias_ref[...]), rest], axis=1)
    tile = jnp.concatenate([rows[:HALF], rows[HALF:]], axis=1)
    tile_ref[...] = jnp.broadcast_to(tile[None], (GRID, HALF, LANES))


def halves(tiles):
    return jnp.concatenate([tiles[:, :WIDE], tiles[:, WIDE:]], axis=0)


def table_kernel(unit_ref, coord_ref, table_ref, squashed_ref):
    units = halves(unit_ref[...])
    pre_act = units[:, NH:NH + 1] * coord_ref[...] + units[:, NH + 1:NH + 2]
    hidden = jnp.maximum(pre_act, 0.0)
    pre = lax.dot_general(
        units[:, :NH], hidden, TN, precision=PRECISE, preferred_element_type=jnp.float32
    )
    squashed = 1.0 / (1.0 + jnp.exp(-pre))
    squashed_ref[...] = squashed
    table_ref[...] = squashed * (16.0 * LOG2E)


def grad_kernel(unit_ref, coord_ref, squashed_ref, row_ref, col_ref, out_ref, *, scale):
    units = halves(unit_ref[...])
    coords = coord_ref[...]
    pre_act = units[:, NH:NH + 1] * coords + units[:, NH + 1:NH + 2]
    hidden = jnp.maximum(pre_act, 0.0)
    squashed = squashed_ref[...]
    pre_grad = (row_ref[...] + col_ref[...]) * scale * 16.0 * squashed * (1.0 - squashed)
    grad_out = lax.dot_general(
        hidden, pre_grad, NT, precision=PRECISE, preferred_element_type=jnp.float32
    )
    back = lax.dot_general(
        units[:, :NH], pre_grad, NN, precision=PRECISE, preferred_element_type=jnp.float32
    )
    unit_grad = jnp.where(pre_act > 0, back, 0.0)
    grad_in = jnp.sum(unit_grad * coords, axis=1, keepdims=True)
    grad_bias = jnp.sum(unit_grad, axis=1, keepdims=True)
    rest = jnp.zeros((HM, WIDE - NH - 2), jnp.float32)
    rows = jnp.concatenate([grad_out, grad_in, grad_bias, rest], axis=1)
    out_ref[...] = jnp.concatenate([rows[:HM // 2], rows[HM // 2:]], axis=1)


def unpack_kernel(got_ref, out_ref, in_ref, bias_ref):
    units = halves(jnp.sum(got_ref[...], axis=0))
    out_ref[...] = units[:, :NH]
    i = lax.broadcasted_iota(jnp.int32, (UNITS, UNITS), 0)
    j = lax.broadcasted_iota(jnp.int32, (UNITS, UNITS), 1)
    for lane, ref in ((NH, in_ref), (NH + 1, bias_ref)):
        spread = jnp.broadcast_to(units[:, lane:lane + 1], (UNITS, UNITS))
        ref[...] = jnp.sum(jnp.where(i == j, spread, 0.0), axis=0, keepdims=True)


def gather_units(mlp_in, mlp_bias, mlp_out):
    tiles = pl.pallas_call(
        pack_kernel, out_shape=jax.ShapeDtypeStruct((GRID, HALF, LANES), jnp.float32)
    )(mlp_in[None], mlp_bias[None], mlp_out)
    got = lax.all_to_all(tiles, "grid", 0, 0, tiled=True)
    return got.reshape(HM // 2, LANES)


def unit_grads(units, coords, squashed, row_table, col_table, scale):
    return pl.pallas_call(
        functools.partial(grad_kernel, scale=scale),
        out_shape=jax.ShapeDtypeStruct((HM // 2, LANES), jnp.float32),
    )(units, coords, squashed, row_table, col_table)


def reduce_units(grads):
    got = lax.all_to_all(grads.reshape(GRID, HALF, LANES), "grid", 0, 0, tiled=True)
    own = jnp.broadcast_to(jnp.sum(got, axis=0)[None], (DP, HALF, LANES))
    got = lax.all_to_all(own, "dp", 0, 0, tiled=True)
    row = jax.ShapeDtypeStruct((1, UNITS), jnp.float32)
    grad_out, grad_in, grad_bias = pl.pallas_call(
        unpack_kernel, out_shape=[jax.ShapeDtypeStruct((UNITS, NH), jnp.float32), row, row]
    )(got)
    return grad_out, grad_in[0], grad_bias[0]


def along_x(step, swap):
    return [(i, ((i // 2 + step) % 4) * 2 + ((i % 2) ^ swap)) for i in range(DP)]


def order_kernel(swap_ref, mine_ref, other_ref, out_ref, *, parts):
    size = mine_ref.shape[0] // parts
    for first, (a_ref, b_ref) in ((0, (mine_ref, other_ref)), (1, (other_ref, mine_ref))):

        @pl.when(swap_ref[0] == first)
        def _():
            for j in range(parts):
                own = slice(j * size, (j + 1) * size)
                out_ref[2 * j * size:(2 * j + 1) * size] = a_ref[own]
                out_ref[(2 * j + 1) * size:(2 * j + 2) * size] = b_ref[own]


def in_order(mine, other, swap, parts):
    rows = mine.shape[0]
    return pl.pallas_call(
        functools.partial(order_kernel, parts=parts),
        in_specs=[pl.BlockSpec(memory_space=pltpu.SMEM)] + [pl.BlockSpec(memory_space=pltpu.VMEM)] * 2,
        out_specs=pl.BlockSpec(memory_space=pltpu.VMEM),
        out_shape=jax.ShapeDtypeStruct((2 * rows, D), jnp.bfloat16),
        compiler_params=pltpu.CompilerParams(vmem_limit_bytes=8 << 20),
        cost_estimate=pl.CostEstimate(flops=0, transcendentals=0, bytes_accessed=8 * rows * D),
    )(swap[None].astype(jnp.int32), mine, other)


def fetch_weight(w_value):
    here = lax.axis_index("grid")
    part = w_value
    for bit, parts in ((2, 1), (0, 2), (1, 2), (3, 1), (4, 1)):
        other = lax.ppermute(part, "grid", [(g, g ^ (1 << bit)) for g in range(GRID)])
        part = in_order(part, other, (here >> bit) & 1, parts)
    mine = [part]
    for step in (1, 2, 3):
        mine.append(lax.ppermute(part, "dp", along_x(step, 0)))
    other = []
    for step in range(4):
        other.append(lax.ppermute(mine[step], "dp", along_x(0, 1)))
    here = lax.axis_index("dp")
    x, core = here // 2, here % 2
    order = (x - jnp.arange(4)) % 4 * 2
    starts = jnp.concatenate([order + core, order + (1 - core)]) * (D // DP)
    return assemble(mine + other, starts.astype(jnp.int32))


def shards(
    q_row, k_row, v_row, q_col, k_col, cotangent, w_value,
    row_positions, col_positions, mlp_in, mlp_bias, mlp_out,
):
    images = q_row.shape[0]
    row_count = q_row.shape[1]
    col_count = q_col.shape[2]
    units = gather_units(mlp_in, mlp_bias, mlp_out)
    coords = jnp.pad(offset_coords(), (0, 2 * LANES - NOFF))[None]
    whole_weight = fetch_weight(w_value)

    rows = lambda x: x.reshape(images * row_count, G, D)
    cols = lambda x: x.transpose(0, 2, 1, 3).reshape(images * col_count, G, D)
    p_row, row_out, table, squashed = row_forward(
        rows(q_row), rows(k_row), rows(v_row), units, coords, col_positions[None]
    )
    col_out = lax.all_to_all(row_out, "grid", split_axis=0, concat_axis=0, tiled=True)

    grad_cols = cols(cotangent)
    p_col, d_values = col_forward(cols(q_col), cols(k_col), grad_cols, table, row_positions[None])
    d_values = d_values.reshape(images, col_count, G, D)
    d_rows = lax.all_to_all(d_values, "grid", split_axis=2, concat_axis=1, tiled=True)

    col_tokens = col_out.reshape(GRID, col_count, images, row_count, D).transpose(2, 1, 0, 3, 4)
    col_tokens = col_tokens.reshape(-1, D)
    value_cols = jnp.dot(
        col_tokens, whole_weight, preferred_element_type=jnp.float32
    ).astype(jnp.bfloat16).reshape(images * col_count, G, D)
    attended, col_table = attention_backward(
        p_col, value_cols, grad_cols, row_positions[None], True
    )
    attended = attended.reshape(images, col_count, G, D).transpose(0, 2, 1, 3)

    d_flat = lax.dot_general(
        d_rows.transpose(0, 2, 1, 3).reshape(-1, D), whole_weight, NT,
        preferred_element_type=jnp.float32,
    )
    d_row_out = d_flat.astype(jnp.bfloat16).reshape(images * row_count, G, D)
    (row_table,) = attention_backward(
        p_row, rows(v_row), d_row_out, col_positions[None], False
    )

    batch_size = lax.axis_size("dp") * images
    grads = unit_grads(units, coords, squashed, row_table, col_table, 1.0 / (batch_size * G))
    grad_mlp_out, grad_mlp_in, grad_mlp_bias = reduce_units(grads)
    return (attended, grad_mlp_in, grad_mlp_bias, grad_mlp_out)


def solution(mesh):
    return jax.shard_map(
        shards,
        mesh=mesh,
        in_specs=(
            P("dp", "grid", None, None),
            P("dp", "grid", None, None),
            P("dp", "grid", None, None),
            P("dp", None, "grid", None),
            P("dp", None, "grid", None),
            P("dp", None, "grid", None),
            P(("dp", "grid"), None),
            P(),
            P(),
            P("grid"),
            P("grid"),
            P("grid", None),
        ),
        out_specs=(P("dp", None, "grid", None), P("grid"), P("grid"), P("grid", None)),
        check_vma=False,
    )
```
